32 devices in a mesh: dom: 2 (over x), tok: 16 (over z, y, core).
Axes of the slice: x: 2, y: 2, z: 4, core: 2. Of those that a mesh axis runs over, the one named last changes fastest.
Arguments:
- tokens: bfloat16 [512, 4096], P(('dom', 'tok')), parts along dimension 0, may hold values from -6 to 6
- rotation_flip: int32 [4096], replicated, may hold values from 0 to 1
- gate_up: bfloat16 [4, 4096, 16384], P('dom', None, 'tok'), parts along dimension 0, may hold values from -0.09375 to 0.09375
- quant_codes: bfloat16 [4, 4096, 16384], P('dom', None, 'tok'), parts along dimension 0, may hold values from -7 to 7
- quant_exps: int32 [4, 32, 16384], P('dom', None, 'tok'), parts along dimension 0, may hold values from -10 to -7
- down_rows: bfloat16 [32768, 4096], P(('dom', 'tok')), parts along dimension 0, may hold values from -0.046875 to 0.046875
Outputs:
- correction: bfloat16 [32768, 4096], P(('dom', 'tok')), parts along dimension 0
The draws below stay inside these ranges and needn't reach their ends.
There are 2 independent parts, one for each index of `dom`. The reference program is written for one: setup_inputs(seed, part) draws one part's arguments, and reference() takes and returns one part's arrays. A program takes and returns all parts, laid end to end along the dimension named above; an argument that names none is the same for every part. Nothing has to cross between parts.
All inputs are finite; a program needn't handle non-finite values.
Results may differ from the reference program's by a relative error of at most 0.012.
Values may be sent and summed in bfloat16 or wider, within the bound.
No kernel may reach another device: no remote copies, remote signals or barrier semaphores. Data moves between devices by JAX's collectives and lax.ppermute only.
A program may use at most 128 MiB of HBM per device.

```python
import jax
import jax.numpy as jnp
from jax import lax

D = 4096
FF = 16384
DO = 4096
GROUP = 128
TOKENS = 256


def draw_quant_codes(key, part):
    return jax.random.randint(key, (2, D, FF), -7, 8).astype(jnp.float32).astype(jnp.bfloat16)


def set_ends(values, key, low, largest):
    spot = [jax.random.randint(jax.random.fold_in(key, axis), (), 0, length) for axis, length in enumerate(values.shape)]
    widest = values.shape.index(max(values.shape))
    neighbour = spot[:widest] + [(spot[widest] + 1) % values.shape[widest]] + spot[widest + 1:]
    return values.at[tuple(spot)].set(low).at[tuple(neighbour)].set(largest)


def block_scale(own_key, dims, cuts, least, largest):
    def one(dim, blocks):
        steps = jax.random.uniform(jax.random.fold_in(jax.random.fold_in(own_key, 6), dim), (blocks,), jnp.float32, least / len(cuts), largest / len(cuts))
        return jnp.repeat(jnp.exp(steps), dims[dim] // blocks).reshape((-1,) + (1,) * (len(dims) - dim - 1))

    factor_of = one(*cuts[0])
    for cut in cuts[1:]:
        factor_of = factor_of * one(*cut)
    return factor_of


def gaussian(own_key, dims, scale, limit, shards=(), held_as=jnp.bfloat16):
    array = scale * jax.random.normal(own_key, dims, jnp.float32)
    if shards:
        array = array * block_scale(own_key, dims, shards, -0.22, 0.18)
    return jnp.clip(array, -limit, limit).astype(held_as)


def setup_inputs(seed: int = 0, part: int = 0) -> dict:
    splits = jax.random.split(jax.random.key(seed), 7)
    part_keys = jax.random.split(jax.random.fold_in(splits[6], part), 7)
    return {
        "tokens": gaussian(part_keys[0], (TOKENS, D), 1.0, 6.0, ((0, 16),)),
        "rotation_flip": set_ends(jax.random.randint(splits[1], (D,), 0, 2), jax.random.fold_in(splits[1], 1), 0, 1).astype(jnp.int32),
        "gate_up": gaussian(part_keys[2], (2, D, FF), D ** -0.5, 0.09375, ((2, 16),)),
        "quant_codes": draw_quant_codes(jax.random.fold_in(jax.random.fold_in(splits[6], part), 71), part),
        "quant_exps": set_ends(jax.random.randint(part_keys[4], (2, D // GROUP, FF), -10, -6), jax.random.fold_in(part_keys[4], 1), -10, (-6) - 1).astype(jnp.int32),
        "down_rows": gaussian(part_keys[5], (FF, DO), FF ** -0.5, 0.046875, ((0, 16),)),
    }


def hadamard_table(order):
    index = jnp.arange(order, dtype=jnp.int32)
    common = index[:, None] & index[None, :]
    parity = jnp.zeros((order, order), jnp.int32)
    for bit_pos in range(max(order.bit_length() - 1, 1)):
        parity = parity ^ ((common >> bit_pos) & 1)
    return (1 - 2 * parity).astype(jnp.float32)


def rotate(inputs, flip):
    width = inputs.shape[-1]
    signed = inputs.astype(jnp.float32) * (1 - 2 * flip).astype(jnp.float32)
    power = width.bit_length() - 1
    outer_len = 2 ** (power // 2)
    inner_len = width // outer_len
    blocks = signed.reshape(-1, outer_len, inner_len)
    mixed = jnp.einsum("ab,nbc,cd->nad", hadamard_table(outer_len), blocks, hadamard_table(inner_len), precision=lax.Precision.HIGHEST)
    return (mixed.reshape(-1, width) * (1.0 / (width ** 0.5))).astype(jnp.bfloat16)


def dequant(codes, exps):
    groups = exps.shape[1]
    scales = jnp.exp2(exps.astype(jnp.float32))
    shaped = codes.astype(jnp.float32).reshape(2, groups, codes.shape[1] // groups, codes.shape[2])
    return (shaped * scales[:, :, None, :]).reshape(codes.shape).astype(jnp.bfloat16)


def swiglu(inputs, weights):
    gate = jnp.dot(inputs, weights[0], preferred_element_type=jnp.float32)
    upper = jnp.dot(inputs, weights[1], preferred_element_type=jnp.float32)
    return (jax.nn.silu(gate) * upper).astype(jnp.bfloat16)


def reference(tokens, rotation_flip, gate_up, quant_codes, quant_exps, down_rows):
    rotated = rotate(tokens, rotation_flip)
    quant_weight = dequant(quant_codes, quant_exps)
    hid_full = swiglu(tokens, gate_up)
    hid_quant = swiglu(rotated, quant_weight)
    mismatch = (hid_full.astype(jnp.float32) - hid_quant.astype(jnp.float32)).astype(jnp.bfloat16)
    projected = jnp.dot(mismatch, down_rows, preferred_element_type=jnp.float32).astype(jnp.bfloat16)
    gram = lax.dot_general(hid_quant, projected, (((0,), (0,)), ((), ())), preferred_element_type=jnp.float32)
    return (gram * (1.0 / (tokens.shape[0] ** 0.5))).astype(jnp.bfloat16)
```

```python
import functools

import jax
import jax.numpy as jnp
from jax import lax
from jax.experimental import pallas as pl
from jax.experimental.pallas import tpu as pltpu
from jax.sharding import PartitionSpec as P

F32 = jnp.float32
BF16 = jnp.bfloat16


def hadamard_table(order):
    index = jnp.arange(order, dtype=jnp.int32)
    common = index[:, None] & index[None, :]
    parity = jnp.zeros((order, order), jnp.int32)
    for bit_pos in range(max(order.bit_length() - 1, 1)):
        parity = parity ^ common >> bit_pos & 1
    return (1 - 2 * parity).astype(F32)


def rotate_kernel(inner, x_ref, flip_ref, table_ref, o_ref):
    width = x_ref.shape[1]
    sign = (1 - 2 * flip_ref[...]).astype(F32).astype(BF16)
    table = table_ref[...]
    parts = [
        jnp.dot(
            x_ref[:, k : k + inner] * sign[:, k : k + inner], table, preferred_element_type=F32
        )
        for k in range(0, width, inner)
    ]
    span = 1
    while span < len(parts):
        for k in range(len(parts)):
            if not k & span:
                a, b = parts[k], parts[k + span]
                parts[k], parts[k + span] = a + b, a - b
        span *= 2
    for k, part in enumerate(parts):
        o_ref[:, k * inner : (k + 1) * inner] = (part * (1.0 / width**0.5)).astype(BF16)


def rotate(x, flip):
    rows, width = x.shape
    inner = min(256, width)
    step = min(64, rows)
    return pl.pallas_call(
        functools.partial(rotate_kernel, inner),
        grid=(rows // step,),
        in_specs=[
            pl.BlockSpec((step, width), lambda i: (i, 0)),
            pl.BlockSpec((1, width), lambda i: (0, 0)),
            pl.BlockSpec((inner, inner), lambda i: (0, 0)),
        ],
        out_specs=pl.BlockSpec((step, width), lambda i: (i, 0)),
        out_shape=jax.ShapeDtypeStruct((rows, width), BF16),
        name="rotate",
    )(x, flip.reshape(1, width), hadamard_table(inner).astype(BF16))


def hidden_kernel(tok_ref, rot_ref, gu_ref, qc_ref, qe_ref, hq_ref, mm_ref):
    tok = tok_ref[...]
    rot = rot_ref[...]
    groups, width = qe_ref.shape[1:]
    gate = jnp.dot(tok, gu_ref[0], preferred_element_type=F32)
    upper = jnp.dot(tok, gu_ref[1], preferred_element_type=F32)
    full = (gate / (1.0 + jnp.exp(-gate)) * upper).astype(BF16)

    def weight(i):
        scale = jnp.exp2(qe_ref[i].astype(F32)).astype(BF16)
        codes = qc_ref[i].reshape(groups, -1, width)
        return (codes * scale[:, None, :]).reshape(-1, width)

    gate = jnp.dot(rot, weight(0), preferred_element_type=F32)
    upper = jnp.dot(rot, weight(1), preferred_element_type=F32)
    quant = (gate / (1.0 + jnp.exp(-gate)) * upper).astype(BF16)
    hq_ref[...] = quant
    mm_ref[...] = (full.astype(F32) - quant.astype(F32)).astype(BF16)


def hidden(tok, rot, gate_up, codes, exps):
    rows, depth = tok.shape
    units = gate_up.shape[2]
    groups = exps.shape[1]
    step = min(256, units)
    flops = 8 * rows * depth * units
    size = 2 * (4 * depth * units + 2 * rows * depth + 2 * rows * units)
    return pl.pallas_call(
        hidden_kernel,
        grid=(units // step,),
        in_specs=[
            pl.BlockSpec((rows, depth), lambda i: (0, 0)),
            pl.BlockSpec((rows, depth), lambda i: (0, 0)),
            pl.BlockSpec((2, depth, step), lambda i: (0, 0, i)),
            pl.BlockSpec((2, depth, step), lambda i: (0, 0, i)),
            pl.BlockSpec((2, groups, step), lambda i: (0, 0, i)),
        ],
        out_specs=[pl.BlockSpec((rows, step), lambda i: (0, i))] * 2,
        out_shape=[jax.ShapeDtypeStruct((rows, units), BF16)] * 2,
        compiler_params=pltpu.CompilerParams(vmem_limit_bytes=50 << 20),
        cost_estimate=pl.CostEstimate(flops=flops, transcendentals=0, bytes_accessed=size),
        name="hidden",
    )(tok, rot, gate_up, codes, exps)


def project_kernel(mm_ref, down_ref, keep_ref, send_ref):
    total = jnp.dot(mm_ref[...], down_ref[...], preferred_element_type=F32)
    half = keep_ref.shape[0]
    keep_ref[...] = total[:half]
    send_ref[...] = total[half:].astype(BF16)


def project(mm, down):
    rows, units = mm.shape
    out = down.shape[1]
    step = min(512, out)
    return pl.pallas_call(
        project_kernel,
        grid=(out // step,),
        in_specs=[
            pl.BlockSpec((rows, units), lambda i: (0, 0)),
            pl.BlockSpec((units, step), lambda i: (0, i)),
        ],
        out_specs=[pl.BlockSpec((rows // 2, step), lambda i: (0, i))] * 2,
        out_shape=[
            jax.ShapeDtypeStruct((rows // 2, out), F32),
            jax.ShapeDtypeStruct((rows // 2, out), BF16),
        ],
        name="project",
    )(mm, down)


def gram_kernel(scale, hq_ref, proj_ref, o_ref):
    gram = lax.dot_general(
        hq_ref[...], proj_ref[...], (((0,), (0,)), ((), ())), preferred_element_type=F32
    )
    o_ref[...] = (gram * scale).astype(BF16)


def gram(hq, projected):
    rows, units = hq.shape
    out = projected.shape[1]
    step = min(256, units)
    return pl.pallas_call(
        functools.partial(gram_kernel, 1.0 / rows**0.5),
        grid=(units // step,),
        in_specs=[
            pl.BlockSpec((rows, step), lambda i: (0, i)),
            pl.BlockSpec((rows, out), lambda i: (0, 0)),
        ],
        out_specs=pl.BlockSpec((step, out), lambda i: (i, 0)),
        out_shape=jax.ShapeDtypeStruct((units, out), BF16),
        name="gram",
    )(hq, projected)


def grid_of(mesh):
    devices = mesh.devices.reshape(-1, mesh.shape["tok"])[0]
    spots = [tuple(d.coords) for d in devices]
    cores = sum(spot == spots[0] for spot in spots)
    chips = spots[::cores]
    side = next((k for k in range(1, len(chips)) if chips[k][2] != chips[0][2]), len(chips))
    if len(chips) % side:
        side = 1
    return len(chips) // side, side, cores


def shift(grid, axis, by):
    pairs = []
    for line in range(grid[0]):
        for side in range(grid[1]):
            for core in range(grid[2]):
                spot = [line, side, core]
                source = (spot[0] * grid[1] + spot[1]) * grid[2] + spot[2]
                spot[axis] = (spot[axis] + by) % grid[axis]
                pairs.append((source, (spot[0] * grid[1] + spot[1]) * grid[2] + spot[2]))
    return pairs


def gather(grid, block):
    send = lambda value, axis, by: lax.ppermute(value, "tok", shift(grid, axis, by))
    order = sorted(range(grid[0]), key=lambda s: min(s, grid[0] - s))
    lines = {s: (block if s == 0 else send(block, 0, s)) for s in order}
    pieces = [lines[s] for s in range(grid[0])]
    near = list(pieces)
    for by in range(1, grid[1]):
        moved = {s: send(lines[s], 1, by) for s in order}
        pieces = pieces + [moved[s] for s in range(grid[0])]
    del near
    mine = jnp.concatenate(pieces, axis=0)
    others = [send(mine, 2, by) for by in range(1, grid[2])]
    return jnp.concatenate([mine] + others, axis=0)


def reduce_to_owner(grid, keep, send_half, rows):
    send = lambda value, axis, by: lax.ppermute(value, "tok", shift(grid, axis, -by))
    total = keep + send(send_half, 2, 1).astype(F32)
    block = lambda side, line: total[(side * grid[0] + line) * rows :][:rows]
    order = sorted(range(grid[0]), key=lambda s: -min(s, grid[0] - s))
    arrived = {}
    for line in order:
        value = block(0, line)
        for by in range(1, grid[1]):
            value = value + send(block(by, line).astype(BF16), 1, by).astype(F32)
        if line:
            arrived[line] = send(value.astype(BF16), 0, line)
        else:
            own = value
    for line in order:
        if line:
            own = own + arrived[line].astype(F32)
    return own.astype(BF16)


def solution(mesh):
    grid = grid_of(mesh)

    def per_device(tokens, rotation_flip, gate_up, quant_codes, quant_exps, down_rows):
        piece = gather(grid, tokens)
        rot = rotate(piece, rotation_flip)
        hq, mm = hidden(piece, rot, gate_up, quant_codes, quant_exps)
        keep, other = project(mm, down_rows)
        own = reduce_to_owner(grid, keep, other, tokens.shape[0])
        projected = gather(grid, own)
        return gram(hq, projected)

    placed = (
        P(("dom", "tok"), None),
        P(),
        P("dom", None, "tok"),
        P("dom", None, "tok"),
        P("dom", None, "tok"),
        P(("dom", "tok"), None),
    )
    return jax.shard_map(
        per_device, mesh=mesh, in_specs=placed, out_specs=P(("dom", "tok"), None), check_vma=False
    )
```

```python
import functools
import math

import jax
import jax.numpy as jnp
from jax import lax
from jax.experimental import pallas as pl
from jax.experimental.pallas import tpu as pltpu
from jax.sharding import PartitionSpec as P


F32 = jnp.float32
BF16 = jnp.bfloat16


def hadamard_table(order):
    index = jnp.arange(order, dtype=jnp.int32)
    common = index[:, None] & index[None, :]
    parity = jnp.zeros((order, order), jnp.int32)
    for bit_pos in range(max(order.bit_length() - 1, 1)):
        parity = parity ^ common >> bit_pos & 1
    return (1 - 2 * parity).astype(F32)


def spec(space):
    return pl.BlockSpec(memory_space=space)


def params(mib):
    return pltpu.CompilerParams(vmem_limit_bytes=mib << 20)


def shaped(dims, dtype):
    return jax.ShapeDtypeStruct(tuple(dims), dtype)


def rotate_rows(x_ref, sign, table, o_ref, step):
    rows, width = x_ref.shape
    inner = table.shape[0]

    @pl.loop(0, rows // step)
    def _(block):
        cut = pl.ds(pl.multiple_of(block * step, step), step)
        parts = [
            jnp.dot(
                x_ref[cut, k : k + inner] * sign[:, k : k + inner], table, preferred_element_type=F32
            )
            for k in range(0, width, inner)
        ]
        span = 1
        while span < len(parts):
            for k in range(len(parts)):
                if not k & span:
                    a, b = parts[k], parts[k + span]
                    parts[k], parts[k + span] = a + b, a - b
            span *= 2
        for k, part in enumerate(parts):
            o_ref[cut, k * inner : (k + 1) * inner] = (part * (1.0 / width**0.5)).astype(BF16)


def swiglu(pieces, input_ref, gate_of, upper_of):
    depth = input_ref.shape[1] // pieces
    gate = upper = 0.0
    for k in range(pieces):
        cut = slice(k * depth, (k + 1) * depth)
        inputs = input_ref[:, cut]
        gate = gate + jnp.dot(inputs, gate_of(k, cut), preferred_element_type=F32)
        upper = upper + jnp.dot(inputs, upper_of(k, cut), preferred_element_type=F32)
    return (gate / (1.0 + jnp.exp(-gate)) * upper).astype(BF16)


def hidden_columns(
    block, width, tok_ref, rot_ref, gu_refs, qc_refs, qe_ref, hq_ref, mm_ref, full_first, arrived
):
    depth = tok_ref.shape[1]
    groups = qe_ref.shape[1]
    pieces = math.gcd(groups, 4)
    cut = pl.ds(pl.multiple_of(block * width, width), width)

    def full_weight(i):
        return lambda k, rows: gu_refs[i][rows, cut]

    def quant_weight(i):
        def piece(k, rows):
            exps = qe_ref[i, k * groups // pieces : (k + 1) * groups // pieces, cut]
            scale = jnp.exp2(exps.astype(F32)).astype(BF16)
            columns = cut if qc_refs[i].shape[1] > width else slice(None)
            codes = qc_refs[i][rows, columns].reshape(groups // pieces, depth // groups, width)
            return (codes * scale[:, None, :]).reshape(depth // pieces, width)

        return piece

    if full_first:
        full = swiglu(pieces, tok_ref, full_weight(0), full_weight(1))
        arrived(block)
    quant = swiglu(pieces, rot_ref, quant_weight(0), quant_weight(1))
    if not full_first:
        arrived(block)
        full = swiglu(pieces, tok_ref, full_weight(0), full_weight(1))
    hq_ref[:, cut] = quant
    mm_ref[:, cut] = (full.astype(F32) - quant.astype(F32)).astype(BF16)


def fetch_kernel(_, source, *refs):
    targets, sem = refs[:-1], refs[-1]
    copies = [
        pltpu.make_async_copy(source.at[k], target, sem.at[k]) for k, target in enumerate(targets)
    ]
    for copy in copies:
        copy.start()
    for copy in copies:
        copy.wait()


def fetch(after, weights):
    count = weights.shape[0]
    return pl.pallas_call(
        fetch_kernel,
        in_specs=[spec(pltpu.VMEM), spec(pltpu.HBM)],
        out_specs=[spec(pltpu.VMEM)] * count,
        out_shape=[pltpu.VMEM(weights.shape[1:], weights.dtype)] * count,
        scratch_shapes=[pltpu.SemaphoreType.DMA((count,))],
        compiler_params=params(1),
        cost_estimate=pl.CostEstimate(
            flops=0, transcendentals=0, bytes_accessed=4 * weights.size
        ),
        name="fetch",
    )(after, pltpu.with_memory_space_constraint(weights, pltpu.HBM))


def project(mm_ref, down_ref, keep_ref, send_ref):
    total = jnp.dot(mm_ref[...], down_ref[...], preferred_element_type=F32)
    own = keep_ref.shape[0]
    keep_ref[...] = total[:own]
    send_ref[...] = total[own:].astype(BF16)


def stack(blocks, o_ref):
    rows = blocks[0].shape[0]
    for k, block in enumerate(blocks):
        o_ref[k * rows : (k + 1) * rows, :] = block[...]


def first_kernel(count, *refs):
    blocks, refs = refs[:count], refs[count:]
    flip_ref, table_ref, *qc_refs, qe_ref, gu_hbm = refs[:6]
    hq_ref, mm_ref, *gu_refs = refs[6:10]
    tok_ref, rot_ref, gu_sem = refs[10:]
    units = hq_ref.shape[1]
    step = min(256, units)

    def full(k, block):
        cut = pl.ds(pl.multiple_of(block * step, step), step)
        return pltpu.make_async_copy(
            gu_hbm.at[k, :, cut], gu_refs[k].at[:, cut], gu_sem.at[k, block]
        )

    def full_arrived(block):
        for k in range(2):
            full(k, block).wait()

    for block in range(units // step):
        for k in range(2):
            full(k, block).start()
    stack(blocks, tok_ref)
    sign = (1 - 2 * flip_ref[...]).astype(F32).astype(BF16)
    rotate_rows(tok_ref, sign, table_ref[...], rot_ref, 64)

    @pl.loop(0, units // step)
    def _(block):
        hidden_columns(
            block, step, tok_ref, rot_ref, gu_refs, qc_refs, qe_ref, hq_ref, mm_ref,
            full_first=False, arrived=full_arrived,
        )


def first_hidden(blocks, flip, table, gate_up, codes, exps):
    rows, depth = len(blocks) * blocks[0].shape[0], blocks[0].shape[1]
    units = codes[0].shape[1]
    return pl.pallas_call(
        functools.partial(first_kernel, len(blocks)),
        in_specs=[spec(pltpu.VMEM)] * (len(blocks) + 5) + [spec(pltpu.HBM)],
        out_specs=[spec(pltpu.VMEM)] * 4,
        out_shape=[
            shaped((rows, units), BF16),
            shaped((rows, units), BF16),
            pltpu.VMEM(gate_up.shape[1:], BF16),
            pltpu.VMEM(gate_up.shape[1:], BF16),
        ],
        scratch_shapes=[
            pltpu.VMEM((rows, depth), BF16),
            pltpu.VMEM((rows, depth), BF16),
            pltpu.SemaphoreType.DMA((2, units // min(256, units))),
        ],
        compiler_params=params(4 + (2 * rows * depth >> 19)),
        cost_estimate=pl.CostEstimate(
            flops=8 * rows * depth * units, transcendentals=0, bytes_accessed=2 * gate_up.size
        ),
        name="first_hidden",
    )(
        *blocks, flip, table, *codes, exps,
        pltpu.with_memory_space_constraint(gate_up, pltpu.HBM),
    )


def next_kernel(count, parts, *refs):
    blocks, mms, refs = refs[:count], refs[count : count + parts], refs[count + parts :]
    flip_ref, table_ref, *gu_refs, qe_ref, qc_hbm, down_hbm = refs[:7]
    hq_ref, keep_ref, send_ref = refs[7:10]
    keeps, sends = refs[10 : 10 + parts], refs[10 + parts : 10 + 2 * parts]
    tok_ref, rot_ref, mm_ref, qc_ref, down_ref, qc_sem, down_sem = refs[10 + 2 * parts :]
    units = hq_ref.shape[1]
    step = min(256, units)
    slots = qc_ref.shape[0]

    def codes(block):
        cut = pl.ds(pl.multiple_of(block * step, step), step)
        slot = lax.rem(block, slots)
        return pltpu.make_async_copy(qc_hbm.at[:, :, cut], qc_ref.at[slot], qc_sem.at[slot])

    rest = pltpu.make_async_copy(down_hbm, down_ref, down_sem)
    for block in range(min(slots, units // step)):
        codes(block).start()
    stack(blocks, tok_ref)
    sign = (1 - 2 * flip_ref[...]).astype(F32).astype(BF16)
    rotate_rows(tok_ref, sign, table_ref[...], rot_ref, 64)

    @pl.loop(0, units // step)
    def _(block):
        slot = lax.rem(block, slots)
        hidden_columns(
            block, step, tok_ref, rot_ref, gu_refs, [qc_ref.at[slot, k] for k in range(2)],
            qe_ref, hq_ref, mm_ref, full_first=True, arrived=lambda k: codes(k).wait(),
        )

        @pl.when(block + slots < units // step)
        def _():
            codes(block + slots).start()

        @pl.when(block == max(units // step - slots - 1, 0))
        def _():
            rest.start()

    rest.wait()
    project(mm_ref, down_ref, keep_ref, send_ref)
    for own_ref, kept, sent in zip(mms, keeps, sends):
        project(own_ref, down_ref, kept, sent)


def next_hidden(cores, blocks, mms, flip, table, gate_up, codes, exps, down):
    rows, depth = len(blocks) * blocks[0].shape[0], blocks[0].shape[1]
    units, width = down.shape
    own = rows // cores
    step = min(256, units)
    parts = 1 + len(mms)
    return pl.pallas_call(
        functools.partial(next_kernel, len(blocks), len(mms)),
        in_specs=[spec(pltpu.VMEM)] * (len(blocks) + len(mms) + 5) + [spec(pltpu.HBM)] * 2,
        out_specs=[spec(pltpu.VMEM)] * (1 + 2 * parts),
        out_shape=[
            shaped((rows, units), BF16),
            shaped((own, width), F32),
            shaped((rows - own, width), BF16),
        ]
        + [shaped((own, width), F32)] * len(mms)
        + [shaped((rows - own, width), BF16)] * len(mms),
        scratch_shapes=[
            pltpu.VMEM((rows, depth), BF16),
            pltpu.VMEM((rows, depth), BF16),
            pltpu.VMEM((rows, units), BF16),
            pltpu.VMEM((2, 2, depth, step), BF16),
            pltpu.VMEM(down.shape, BF16),
            pltpu.SemaphoreType.DMA((2,)),
            pltpu.SemaphoreType.DMA(()),
        ],
        compiler_params=params(2 + (2 * rows * depth + 4 * depth * step + down.size >> 19)),
        cost_estimate=pl.CostEstimate(
            flops=10 * rows * depth * units, transcendentals=0, bytes_accessed=2 * codes.size
        ),
        name="next_hidden",
    )(
        *blocks, *mms, flip, table, *gate_up, exps,
        pltpu.with_memory_space_constraint(codes, pltpu.HBM),
        pltpu.with_memory_space_constraint(down, pltpu.HBM),
    )


def last_kernel(mm_ref, down_ref, keep_ref, send_ref):
    project(mm_ref, down_ref, keep_ref, send_ref)


def last_project(cores, mm, down):
    rows, (units, width) = mm.shape[0], down.shape
    own = rows // cores
    return pl.pallas_call(
        last_kernel,
        in_specs=[spec(pltpu.VMEM)] * 2,
        out_specs=[spec(pltpu.VMEM)] * 2,
        out_shape=[shaped((own, width), F32), shaped((rows - own, width), BF16)],
        compiler_params=params(12),
        name="last_project",
    )(mm, down)


def join_kernel(others, keep_ref, *refs):
    received, outs = refs[:others], refs[others:]
    rows = outs[0].shape[0]
    for k, out in enumerate(outs):
        cut = slice(k * rows, (k + 1) * rows)
        total = keep_ref[cut, :]
        for ref in received:
            total = total + ref[cut, :].astype(F32)
        out[...] = total.astype(BF16)


def join(lines, keep, received):
    rows = keep.shape[0] // lines
    block = shaped((rows, keep.shape[1]), BF16)
    return pl.pallas_call(
        functools.partial(join_kernel, len(received)),
        in_specs=[spec(pltpu.VMEM)] * (1 + len(received)),
        out_specs=[spec(pltpu.VMEM)] * lines,
        out_shape=[block] * lines,
        compiler_params=params(4),
        name="join",
    )(keep, *received)


def add_kernel(cut, whole, keep_ref, *refs):
    received, out = refs[:-1], refs[-1]
    total = keep_ref[cut, :]
    for k, ref in enumerate(received):
        total = total + (ref[cut, :] if k < whole else ref[...]).astype(F32)
    out[...] = total.astype(BF16)


def add(rows, line, keep, received, blocks):
    return pl.pallas_call(
        functools.partial(add_kernel, slice(line * rows, (line + 1) * rows), len(received)),
        in_specs=[spec(pltpu.VMEM)] * (1 + len(received) + len(blocks)),
        out_specs=spec(pltpu.VMEM),
        out_shape=shaped((rows, keep.shape[1]), BF16),
        compiler_params=params(4),
        name="add",
    )(keep, *received, *blocks)


def gram_kernel(scale, parts, *refs):
    hqs, blocks = refs[:parts], refs[parts:-3]
    o_ref, hq_ref, proj_ref = refs[-3:]

    @pl.when(pl.program_id(0) == 0)
    def _():
        stack(hqs, hq_ref)
        stack(blocks, proj_ref)

    step = o_ref.shape[0]
    cut = pl.ds(pl.multiple_of(pl.program_id(0) * step, step), step)
    gram = lax.dot_general(
        hq_ref[:, cut], proj_ref[...], (((0,), (0,)), ((), ())), preferred_element_type=F32
    )
    o_ref[...] = (gram * scale).astype(BF16)


def gram(hqs, blocks):
    rows = len(hqs) * hqs[0].shape[0]
    units, out = hqs[0].shape[1], blocks[0].shape[1]
    step = min(128, units)
    return pl.pallas_call(
        functools.partial(gram_kernel, 1.0 / rows**0.5, len(hqs)),
        grid=(units // step,),
        in_specs=[spec(pltpu.VMEM)] * (len(hqs) + len(blocks)),
        out_specs=pl.BlockSpec((step, out), lambda i: (i, 0)),
        out_shape=shaped((units, out), BF16),
        scratch_shapes=[pltpu.VMEM((rows, units), BF16), pltpu.VMEM((rows, out), BF16)],
        compiler_params=params(16),
        name="gram",
    )(*hqs, *blocks)


def grid_of(mesh):
    devices = mesh.devices.reshape(-1, mesh.shape["tok"])[0]
    spots = [tuple(d.coords) for d in devices]
    cores = sum(spot == spots[0] for spot in spots)
    chips = spots[::cores]
    side = next((k for k in range(1, len(chips)) if chips[k][2] != chips[0][2]), len(chips))
    if len(chips) % side:
        side = 1
    return len(chips) // side, side, cores


def shift(grid, axis, by):
    pairs = []
    for line in range(grid[0]):
        for side in range(grid[1]):
            for core in range(grid[2]):
                spot = [line, side, core]
                source = (spot[0] * grid[1] + spot[1]) * grid[2] + spot[2]
                spot[axis] = (spot[axis] + by) % grid[axis]
                pairs.append((source, (spot[0] * grid[1] + spot[1]) * grid[2] + spot[2]))
    return pairs


def far_first(lines):
    return sorted(range(lines), key=lambda s: -min(s, lines - s))


def gather(grid, block):
    send = lambda value, axis, by: lax.ppermute(value, "tok", shift(grid, axis, by))
    order = far_first(grid[0])[::-1]
    blocks = {}
    for line in order:
        blocks[0, 0, line] = send(block, 0, line) if line else block
    for by in range(grid[1]):
        for line in order:
            if by:
                blocks[by, 0, line] = send(blocks[0, 0, line], 1, by)
            for core in range(1, grid[2]):
                blocks[by, core, line] = send(blocks[by, 0, line], 2, core)
    return blocks, blocks[0, 0, order[1]]


def reduce_to_owner(grid, group, kept, sent):
    send = lambda value, axis, by: lax.ppermute(value, "tok", shift(grid, axis, -by))
    size = kept[0, 0].shape[0]
    rows = size // group
    received = {
        key: [send(sent[key][c * size :][:size], 2, c + 1) for c in range(grid[2] - 1)]
        for key in list(kept)[::-1]
    }
    moved = {line: [] for line in range(grid[0])}
    for by in range(grid[1] - 1, 0, -1):
        blocks = []
        for part in range(grid[0] // group):
            blocks += join(group, kept[by, part], received[by, part])
        for line in far_first(grid[0]):
            moved[line].append(send(blocks[line], 1, by))

    def total(line, arrived):
        key = 0, line // group
        return add(rows, line % group, kept[key], received[key], moved[line] + arrived)

    arrived = [send(total(line, []), 0, line) for line in far_first(grid[0])[:-1]]
    return total(0, arrived)


def solution(mesh):
    grid = grid_of(mesh)
    group = math.gcd(grid[0], 4)
    chunks = [(by, part) for by in range(grid[1]) for part in range(grid[0] // group)]

    def chunk_blocks(blocks, chunk):
        by, part = chunk
        lines = range(part * group, (part + 1) * group)
        return [blocks[by, core, line] for core in range(grid[2]) for line in lines]

    def per_device(tokens, rotation_flip, gate_up, quant_codes, quant_exps, down_rows):
        width = tokens.shape[1]
        held = lambda value: pltpu.with_memory_space_constraint(value, pltpu.VMEM)
        flip = rotation_flip.reshape(1, width)
        table = hadamard_table(min(256, width)).astype(BF16)
        blocks, near = gather(grid, tokens)
        codes = [held(value) for value in fetch(near, quant_codes)]
        hq, mm, *gu = first_hidden(
            chunk_blocks(blocks, chunks[0]), flip, table, gate_up, codes, quant_exps
        )
        gu = [held(value) for value in gu]
        hqs, kept, sent = [hq], {chunks[0]: None}, {}
        for chunk in chunks[1:]:
            hq, kept[chunk], sent[chunk], *rest = next_hidden(
                grid[2],
                chunk_blocks(blocks, chunk),
                [mm] if chunk == chunks[-1] else [],
                flip, table, gu, quant_codes, quant_exps, down_rows,
            )
            hqs.append(hq)
        if len(chunks) == 1:
            rest = last_project(grid[2], mm, down_rows)
        kept[chunks[0]], sent[chunks[0]] = rest
        own = reduce_to_owner(grid, group, kept, sent)
        projected, _ = gather(grid, own)
        return gram(hqs, sum((chunk_blocks(projected, chunk) for chunk in chunks), []))

    placed = (
        P(("dom", "tok"), None),
        P(),
        P("dom", None, "tok"),
        P("dom", None, "tok"),
        P("dom", None, "tok"),
        P(("dom", "tok"), None),
    )
    return jax.shard_map(
        per_device, mesh=mesh, in_specs=placed, out_specs=P(("dom", "tok"), None), check_vma=False
    )
```

```python
import functools
import math

import jax
import jax.numpy as jnp
from jax import lax
from jax.experimental import pallas as pl
from jax.experimental.pallas import tpu as pltpu
from jax.sharding import PartitionSpec as P


F32 = jnp.float32
BF16 = jnp.bfloat16


def hadamard_table(order):
    index = jnp.arange(order, dtype=jnp.int32)
    common = index[:, None] & index[None, :]
    parity = jnp.zeros((order, order), jnp.int32)
    for bit_pos in range(max(order.bit_length() - 1, 1)):
        parity = parity ^ common >> bit_pos & 1
    return (1 - 2 * parity).astype(F32)


def spec(space):
    return pl.BlockSpec(memory_space=space)


def params(mib):
    return pltpu.CompilerParams(vmem_limit_bytes=mib << 20)


def shaped(dims, dtype):
    return jax.ShapeDtypeStruct(tuple(dims), dtype)


def stack(blocks, o_ref):
    rows = blocks[0].shape[0]
    for k, block in enumerate(blocks):
        o_ref[k * rows : (k + 1) * rows, :] = block[...]


def rotate_rows(blocks, sign, table, x_ref, mixed_ref, o_ref):
    stack(blocks, x_ref)
    rows, width = x_ref.shape
    inner = table.shape[0]
    count = width // inner
    scale = 1.0 / width**0.5
    signed = jnp.concatenate(
        [x_ref[:, k : k + inner] * sign[:, k : k + inner] for k in range(0, width, inner)], axis=0
    )
    mixed_ref[...] = jnp.dot(signed, table, preferred_element_type=F32)
    step = 16

    @pl.loop(0, rows // step)
    def _(block):
        row = pl.multiple_of(block * step, step)
        parts = [mixed_ref[pl.ds(k * rows + row, step), :] for k in range(count)]
        span = 1
        while span < count:
            for k in range(count):
                if not k & span:
                    a, b = parts[k], parts[k + span]
                    parts[k], parts[k + span] = a + b, a - b
            span *= 2
        for k, part in enumerate(parts):
            o_ref[pl.ds(row, step), k * inner : (k + 1) * inner] = (part * scale).astype(BF16)


def swiglu(pieces, input_ref, gate_of, upper_of):
    depth = input_ref.shape[1] // pieces
    gate = upper = 0.0
    for k in range(pieces):
        cut = slice(k * depth, (k + 1) * depth)
        inputs = input_ref[:, cut]
        gate = gate + jnp.dot(inputs, gate_of(k, cut), preferred_element_type=F32)
        upper = upper + jnp.dot(inputs, upper_of(k, cut), preferred_element_type=F32)
    return (gate / (1.0 + jnp.exp(-gate)) * upper).astype(BF16)


def depth_pieces(groups):
    return math.gcd(groups, 4)


def hidden_columns(
    block, width, tok_ref, rot_ref, gu_refs, codes_of, qe_ref, hq_ref, mm_ref, full_first, arrived
):
    depth = tok_ref.shape[1]
    groups = qe_ref.shape[1]
    pieces = depth_pieces(groups)
    cut = pl.ds(pl.multiple_of(block * width, width), width)

    def full_weight(i):
        return lambda k, rows: gu_refs[i][rows, cut]

    def quant_weight(i):
        def piece(k, rows):
            exps = qe_ref[i, k * groups // pieces : (k + 1) * groups // pieces, cut]
            scale = jnp.exp2(exps.astype(F32)).astype(BF16)
            codes = codes_of(i, k, rows, cut).reshape(groups // pieces, depth // groups, width)
            return (codes * scale[:, None, :]).reshape(depth // pieces, width)

        return piece

    if full_first:
        full = swiglu(pieces, tok_ref, full_weight(0), full_weight(1))
        arrived(block)
    quant = swiglu(pieces, rot_ref, quant_weight(0), quant_weight(1))
    if not full_first:
        arrived(block)
        full = swiglu(pieces, tok_ref, full_weight(0), full_weight(1))
    hq_ref[:, cut] = quant
    mm_ref[:, cut] = (full.astype(F32) - quant.astype(F32)).astype(BF16)


def fetch_kernel(_, source, *refs):
    targets, sem = refs[:-1], refs[-1]
    rows = targets[0].shape[0]
    pieces = source.shape[1] // rows
    copies = [
        pltpu.make_async_copy(
            source.at[k // pieces, pl.ds(k % pieces * rows, rows)], target, sem.at[k]
        )
        for k, target in enumerate(targets)
    ]
    for copy in copies:
        copy.start()
    for copy in copies:
        copy.wait()


def fetch(after, weights, pieces):
    count = weights.shape[0] * pieces
    dims = weights.shape[1] // pieces, weights.shape[2]
    return pl.pallas_call(
        fetch_kernel,
        in_specs=[spec(pltpu.VMEM), spec(pltpu.HBM)],
        out_specs=[spec(pltpu.VMEM)] * count,
        out_shape=[pltpu.VMEM(dims, weights.dtype)] * count,
        scratch_shapes=[pltpu.SemaphoreType.DMA((count,))],
        compiler_params=params(1),
        cost_estimate=pl.CostEstimate(
            flops=0, transcendentals=0, bytes_accessed=4 * weights.size
        ),
        name="fetch",
    )(after, pltpu.with_memory_space_constraint(weights, pltpu.HBM))


def project(mm_ref, down_ref, keep_ref, send_ref):
    total = jnp.dot(mm_ref[...], down_ref[...], preferred_element_type=F32)
    own = keep_ref.shape[0]
    keep_ref[...] = total[:own]
    send_ref[...] = total[own:].astype(BF16)


def first_kernel(count, *refs):
    blocks, refs = refs[:count], refs[count:]
    flip_ref, table_ref, *qc_refs, qe_ref, gu_hbm = refs[:-8]
    hq_ref, mm_ref, *gu_refs = refs[-8:-4]
    tok_ref, rot_ref, mixed_ref, gu_sem = refs[-4:]
    units = hq_ref.shape[1]
    step = min(256, units)

    def full(k, block):
        cut = pl.ds(pl.multiple_of(block * step, step), step)
        return pltpu.make_async_copy(
            gu_hbm.at[k, :, cut], gu_refs[k].at[:, cut], gu_sem.at[k, block]
        )

    def full_arrived(block):
        for k in range(2):
            full(k, block).wait()

    for block in range(units // step):
        for k in range(2):
            full(k, block).start()
    sign = (1 - 2 * flip_ref[...]).astype(F32).astype(BF16)
    rotate_rows(blocks, sign, table_ref[...], tok_ref, mixed_ref, rot_ref)

    @pl.loop(0, units // step)
    def _(block):
        hidden_columns(
            block, step, tok_ref, rot_ref, gu_refs,
            lambda i, k, rows, cut: qc_refs[i * len(qc_refs) // 2 + k][:, cut],
            qe_ref, hq_ref, mm_ref, full_first=False, arrived=full_arrived,
        )


def first_hidden(blocks, flip, table, gate_up, codes, exps):
    rows, depth = len(blocks) * blocks[0].shape[0], blocks[0].shape[1]
    units = codes[0].shape[1]
    return pl.pallas_call(
        functools.partial(first_kernel, len(blocks)),
        in_specs=[spec(pltpu.VMEM)] * (len(blocks) + 3 + len(codes)) + [spec(pltpu.HBM)],
        out_specs=[spec(pltpu.VMEM)] * 4,
        out_shape=[
            shaped((rows, units), BF16),
            shaped((rows, units), BF16),
            pltpu.VMEM(gate_up.shape[1:], BF16),
            pltpu.VMEM(gate_up.shape[1:], BF16),
        ],
        scratch_shapes=[
            pltpu.VMEM((rows, depth), BF16),
            pltpu.VMEM((rows, depth), BF16),
            pltpu.VMEM((rows * depth // table.shape[0], table.shape[0]), F32),
            pltpu.SemaphoreType.DMA((2, units // min(256, units))),
        ],
        compiler_params=params(2 + (4 * rows * depth >> 19)),
        cost_estimate=pl.CostEstimate(
            flops=8 * rows * depth * units, transcendentals=0, bytes_accessed=2 * gate_up.size
        ),
        name="first_hidden",
    )(
        *blocks, flip, table, *codes, exps,
        pltpu.with_memory_space_constraint(gate_up, pltpu.HBM),
    )


def next_kernel(count, *refs):
    blocks, refs = refs[:count], refs[count:]
    flip_ref, table_ref, *gu_refs, qe_ref, down_ref, qc_hbm = refs[:7]
    hq_ref, keep_ref, send_ref = refs[7:10]
    tok_ref, rot_ref, mixed_ref, mm_ref, qc_ref, qc_sem = refs[10:]
    units = hq_ref.shape[1]
    step = min(256, units)

    slots = qc_ref.shape[0]

    def codes(block):
        cut = pl.ds(pl.multiple_of(block * step, step), step)
        slot = lax.rem(block, slots)
        return pltpu.make_async_copy(qc_hbm.at[:, :, cut], qc_ref.at[slot], qc_sem.at[slot])

    for block in range(slots):
        codes(block).start()
    sign = (1 - 2 * flip_ref[...]).astype(F32).astype(BF16)
    rotate_rows(blocks, sign, table_ref[...], tok_ref, mixed_ref, rot_ref)

    @pl.loop(0, units // step)
    def _(block):
        slot = lax.rem(block, slots)
        hidden_columns(
            block, step, tok_ref, rot_ref, gu_refs,
            lambda i, k, rows, cut: qc_ref[slot, i, rows, :],
            qe_ref, hq_ref, mm_ref, full_first=True, arrived=lambda k: codes(k).wait(),
        )

        @pl.when(block + slots < units // step)
        def _():
            codes(block + slots).start()

    project(mm_ref, down_ref, keep_ref, send_ref)


def next_hidden(cores, blocks, flip, table, gate_up, codes, exps, down):
    rows, depth = len(blocks) * blocks[0].shape[0], blocks[0].shape[1]
    units, width = down.shape
    own = rows // cores
    step = min(256, units)
    slots = min(2, units // step)
    return pl.pallas_call(
        functools.partial(next_kernel, len(blocks)),
        in_specs=[spec(pltpu.VMEM)] * (len(blocks) + 6) + [spec(pltpu.HBM)],
        out_specs=[spec(pltpu.VMEM)] * 3,
        out_shape=[
            shaped((rows, units), BF16),
            shaped((own, width), F32),
            shaped((rows - own, width), BF16),
        ],
        scratch_shapes=[
            pltpu.VMEM((rows, depth), BF16),
            pltpu.VMEM((rows, depth), BF16),
            pltpu.VMEM((rows * depth // table.shape[0], table.shape[0]), F32),
            pltpu.VMEM((rows, units), BF16),
            pltpu.VMEM((slots, 2, depth, step), BF16),
            pltpu.SemaphoreType.DMA((slots,)),
        ],
        compiler_params=params(2 + (4 * rows * depth + 2 * slots * depth * step >> 19)),
        cost_estimate=pl.CostEstimate(
            flops=10 * rows * depth * units, transcendentals=0, bytes_accessed=2 * codes.size
        ),
        name="next_hidden",
    )(
        *blocks, flip, table, *gate_up, exps, down,
        pltpu.with_memory_space_constraint(codes, pltpu.HBM),
    )


def last_kernel(mm_ref, down_ref, keep_ref, send_ref):
    project(mm_ref, down_ref, keep_ref, send_ref)


def last_project(cores, mm, down):
    rows, (units, width) = mm.shape[0], down.shape
    own = rows // cores
    return pl.pallas_call(
        last_kernel,
        in_specs=[spec(pltpu.VMEM)] * 2,
        out_specs=[spec(pltpu.VMEM)] * 2,
        out_shape=[shaped((own, width), F32), shaped((rows - own, width), BF16)],
        compiler_params=params(4),
        name="last_project",
    )(mm, down)


def join_kernel(others, keep_ref, *refs):
    received, outs = refs[:others], refs[others:]
    rows = outs[0].shape[0]
    for k, out in enumerate(outs):
        cut = slice(k * rows, (k + 1) * rows)
        total = keep_ref[cut, :]
        for ref in received:
            total = total + ref[cut, :].astype(F32)
        out[...] = total.astype(BF16)


def join(lines, keep, received):
    rows = keep.shape[0] // lines
    block = shaped((rows, keep.shape[1]), BF16)
    return pl.pallas_call(
        functools.partial(join_kernel, len(received)),
        in_specs=[spec(pltpu.VMEM)] * (1 + len(received)),
        out_specs=[spec(pltpu.VMEM)] * lines,
        out_shape=[block] * lines,
        compiler_params=params(4),
        name="join",
    )(keep, *received)


def add_kernel(cut, whole, keep_ref, *refs):
    received, out = refs[:-1], refs[-1]
    total = keep_ref[cut, :]
    for k, ref in enumerate(received):
        total = total + (ref[cut, :] if k < whole else ref[...]).astype(F32)
    out[...] = total.astype(BF16)


def add(rows, line, keep, received, blocks):
    return pl.pallas_call(
        functools.partial(add_kernel, slice(line * rows, (line + 1) * rows), len(received)),
        in_specs=[spec(pltpu.VMEM)] * (1 + len(received) + len(blocks)),
        out_specs=spec(pltpu.VMEM),
        out_shape=shaped((rows, keep.shape[1]), BF16),
        compiler_params=params(4),
        name="add",
    )(keep, *received, *blocks)


def gram_kernel(scale, parts, *refs):
    hqs, blocks = refs[:parts], refs[parts:-6]
    o_hbm, hq_ref, turned_ref, proj_ref, o_ref, sem = refs[-6:]
    stack(hqs, hq_ref)
    stack(blocks, proj_ref)
    turned_ref[...] = hq_ref[...].T
    units = turned_ref.shape[0]
    step = min(256, units)
    copies = []
    for k in range(units // step):
        cut = pl.ds(k * step, step)
        gram = jnp.dot(turned_ref[cut, :], proj_ref[...], preferred_element_type=F32)
        o_ref[cut, :] = (gram * scale).astype(BF16)
        copies.append(pltpu.make_async_copy(o_ref.at[cut], o_hbm.at[cut], sem.at[k]))
        copies[-1].start()
    for copy in copies:
        copy.wait()


def gram(hqs, blocks):
    rows = sum(hq.shape[0] for hq in hqs)
    units, out = hqs[0].shape[1], blocks[0].shape[1]
    return pl.pallas_call(
        functools.partial(gram_kernel, 1.0 / rows**0.5, len(hqs)),
        in_specs=[spec(pltpu.VMEM)] * (len(hqs) + len(blocks)),
        out_specs=spec(pltpu.HBM),
        out_shape=shaped((units, out), BF16),
        scratch_shapes=[
            pltpu.VMEM((rows, units), BF16),
            pltpu.VMEM((units, rows), BF16),
            pltpu.VMEM((rows, out), BF16),
            pltpu.VMEM((units, out), BF16),
            pltpu.SemaphoreType.DMA((units // min(256, units),)),
        ],
        compiler_params=params(24),
        name="gram",
    )(*hqs, *blocks)


def grid_of(mesh):
    devices = mesh.devices.reshape(-1, mesh.shape["tok"])[0]
    spots = [tuple(d.coords) for d in devices]
    cores = sum(spot == spots[0] for spot in spots)
    chips = spots[::cores]
    side = next((k for k in range(1, len(chips)) if chips[k][2] != chips[0][2]), len(chips))
    if len(chips) % side:
        side = 1
    return len(chips) // side, side, cores


def shift(grid, axis, by):
    pairs = []
    for line in range(grid[0]):
        for side in range(grid[1]):
            for core in range(grid[2]):
                spot = [line, side, core]
                source = (spot[0] * grid[1] + spot[1]) * grid[2] + spot[2]
                spot[axis] = (spot[axis] + by) % grid[axis]
                pairs.append((source, (spot[0] * grid[1] + spot[1]) * grid[2] + spot[2]))
    return pairs


def far_first(lines):
    return sorted(range(lines), key=lambda s: -min(s, lines - s))


def gather(grid, block):
    send = lambda value, axis, by: lax.ppermute(value, "tok", shift(grid, axis, by))
    order = far_first(grid[0])[::-1]
    blocks = {}
    for line in order:
        blocks[0, 0, line] = send(block, 0, line) if line else block
    for by in range(grid[1]):
        for line in order:
            if by:
                blocks[by, 0, line] = send(blocks[0, 0, line], 1, by)
            for core in range(1, grid[2]):
                blocks[by, core, line] = send(blocks[by, 0, line], 2, core)
    return blocks, blocks[0, 0, order[1]]


def reduce_to_owner(grid, group, kept, sent):
    send = lambda value, axis, by: lax.ppermute(value, "tok", shift(grid, axis, -by))
    size = kept[0, 0].shape[0]
    rows = size // group
    received = {
        key: [send(sent[key][c * size :][:size], 2, c + 1) for c in range(grid[2] - 1)]
        for key in list(kept)[::-1]
    }
    moved = {line: [] for line in range(grid[0])}
    for by in range(grid[1] - 1, 0, -1):
        blocks = []
        for part in range(grid[0] // group):
            blocks += join(group, kept[by, part], received[by, part])
        for line in far_first(grid[0]):
            moved[line].append(send(blocks[line], 1, by))

    def total(line, arrived):
        key = 0, line // group
        return add(rows, line % group, kept[key], received[key], moved[line] + arrived)

    arrived = [send(total(line, []), 0, line) for line in far_first(grid[0])[:-1]]
    return total(0, arrived)


def solution(mesh):
    grid = grid_of(mesh)
    group = math.gcd(grid[0], 4)
    chunks = [(by, part) for by in range(grid[1]) for part in range(grid[0] // group)]

    def chunk_blocks(blocks, chunk):
        by, part = chunk
        lines = range(part * group, (part + 1) * group)
        return [blocks[by, core, line] for core in range(grid[2]) for line in lines]

    def per_device(tokens, rotation_flip, gate_up, quant_codes, quant_exps, down_rows):
        width = tokens.shape[1]
        held = lambda value: pltpu.with_memory_space_constraint(value, pltpu.VMEM)
        flip = rotation_flip.reshape(1, width)
        table = hadamard_table(min(256, width)).astype(BF16)
        blocks, near = gather(grid, tokens)
        codes = [held(value) for value in fetch(near, quant_codes, depth_pieces(quant_exps.shape[1]))]
        hq, mm, *gu = first_hidden(
            chunk_blocks(blocks, chunks[0]), flip, table, gate_up, codes, quant_exps
        )
        gu = [held(value) for value in gu]
        hqs, kept, sent = [hq], {chunks[0]: None}, {}
        for chunk in chunks[1:]:
            hq, kept[chunk], sent[chunk] = next_hidden(
                grid[2], chunk_blocks(blocks, chunk), flip, table, gu, quant_codes, quant_exps, down_rows
            )
            hqs.append(hq)
        kept[chunks[0]], sent[chunks[0]] = last_project(grid[2], mm, down_rows)
        own = reduce_to_owner(grid, group, kept, sent)
        projected, _ = gather(grid, own)
        return gram(hqs, sum((chunk_blocks(projected, chunk) for chunk in chunks), []))

    placed = (
        P(("dom", "tok"), None),
        P(),
        P("dom", None, "tok"),
        P("dom", None, "tok"),
        P("dom", None, "tok"),
        P(("dom", "tok"), None),
    )
    return jax.shard_map(
        per_device, mesh=mesh, in_specs=placed, out_specs=P(("dom", "tok"), None), check_vma=False
    )
```

```python
import functools
import math

import jax
import jax.numpy as jnp
from jax import lax
from jax.experimental import pallas as pl
from jax.experimental.pallas import tpu as pltpu
from jax.sharding import PartitionSpec as P


F32 = jnp.float32
BF16 = jnp.bfloat16


def hadamard_table(order):
    index = jnp.arange(order, dtype=jnp.int32)
    common = index[:, None] & index[None, :]
    parity = jnp.zeros((order, order), jnp.int32)
    for bit_pos in range(max(order.bit_length() - 1, 1)):
        parity = parity ^ common >> bit_pos & 1
    return (1 - 2 * parity).astype(F32)


def spec(space):
    return pl.BlockSpec(memory_space=space)


def params(mib):
    return pltpu.CompilerParams(vmem_limit_bytes=mib << 20)


def shaped(dims, dtype):
    return jax.ShapeDtypeStruct(tuple(dims), dtype)


def stack(blocks, o_ref):
    rows = blocks[0].shape[0]
    for k, block in enumerate(blocks):
        o_ref[k * rows : (k + 1) * rows, :] = block[...]


def rotate_rows(blocks, sign, table, x_ref, mixed_ref, o_ref):
    stack(blocks, x_ref)
    rows, width = x_ref.shape
    inner = table.shape[0]
    count = width // inner
    scale = 1.0 / width**0.5
    signed = jnp.concatenate(
        [x_ref[:, k : k + inner] * sign[:, k : k + inner] for k in range(0, width, inner)], axis=0
    )
    mixed_ref[...] = jnp.dot(signed, table, preferred_element_type=F32)
    step = 16

    @pl.loop(0, rows // step)
    def _(block):
        row = pl.multiple_of(block * step, step)
        parts = [mixed_ref[pl.ds(k * rows + row, step), :] for k in range(count)]
        span = 1
        while span < count:
            for k in range(count):
                if not k & span:
                    a, b = parts[k], parts[k + span]
                    parts[k], parts[k + span] = a + b, a - b
            span *= 2
        for k, part in enumerate(parts):
            o_ref[pl.ds(row, step), k * inner : (k + 1) * inner] = (part * scale).astype(BF16)


def swiglu(pieces, input_ref, gate_of, upper_of):
    depth = input_ref.shape[1] // pieces
    gate = upper = 0.0
    for k in range(pieces):
        cut = slice(k * depth, (k + 1) * depth)
        inputs = input_ref[:, cut]
        gate = gate + jnp.dot(inputs, gate_of(k, cut), preferred_element_type=F32)
        upper = upper + jnp.dot(inputs, upper_of(k, cut), preferred_element_type=F32)
    return (gate / (1.0 + jnp.exp(-gate)) * upper).astype(BF16)


def depth_pieces(groups):
    return math.gcd(groups, 4)


def hidden_columns(
    block, width, tok_ref, rot_ref, gu_refs, codes_of, qe_ref, hq_ref, mm_ref, full_first, arrived
):
    depth = tok_ref.shape[1]
    groups = qe_ref.shape[1]
    pieces = depth_pieces(groups)
    cut = pl.ds(pl.multiple_of(block * width, width), width)

    def full_weight(i):
        return lambda k, rows: gu_refs[i][rows, cut]

    def quant_weight(i):
        def piece(k, rows):
            exps = qe_ref[i, k * groups // pieces : (k + 1) * groups // pieces, cut]
            scale = jnp.exp2(exps.astype(F32)).astype(BF16)
            codes = codes_of(i, k, rows, cut).reshape(groups // pieces, depth // groups, width)
            return (codes * scale[:, None, :]).reshape(depth // pieces, width)

        return piece

    if full_first:
        full = swiglu(pieces, tok_ref, full_weight(0), full_weight(1))
        arrived(block)
    quant = swiglu(pieces, rot_ref, quant_weight(0), quant_weight(1))
    if not full_first:
        arrived(block)
        full = swiglu(pieces, tok_ref, full_weight(0), full_weight(1))
    hq_ref[:, cut] = quant
    mm_ref[:, cut] = (full.astype(F32) - quant.astype(F32)).astype(BF16)


def fetch_kernel(_, source, *refs):
    targets, sem = refs[:-1], refs[-1]
    rows = targets[0].shape[0]
    pieces = source.shape[1] // rows
    copies = [
        pltpu.make_async_copy(
            source.at[k // pieces, pl.ds(k % pieces * rows, rows)], target, sem.at[k]
        )
        for k, target in enumerate(targets)
    ]
    for copy in copies:
        copy.start()
    for copy in copies:
        copy.wait()


def fetch(after, weights, pieces):
    count = weights.shape[0] * pieces
    dims = weights.shape[1] // pieces, weights.shape[2]
    return pl.pallas_call(
        fetch_kernel,
        in_specs=[spec(pltpu.VMEM), spec(pltpu.HBM)],
        out_specs=[spec(pltpu.VMEM)] * count,
        out_shape=[pltpu.VMEM(dims, weights.dtype)] * count,
        scratch_shapes=[pltpu.SemaphoreType.DMA((count,))],
        compiler_params=params(1),
        cost_estimate=pl.CostEstimate(
            flops=0, transcendentals=0, bytes_accessed=4 * weights.size
        ),
        name="fetch",
    )(after, pltpu.with_memory_space_constraint(weights, pltpu.HBM))


def column_parts(width):
    return 2 if width % 256 == 0 else 1


def project(mm_ref, down_ref, keeps, sends):
    own, columns = keeps[0].shape
    for k, (keep_ref, send_ref) in enumerate(zip(keeps, sends)):
        down = down_ref[:, k * columns : (k + 1) * columns]
        total = jnp.dot(mm_ref[...], down, preferred_element_type=F32)
        keep_ref[...] = total[:own]
        send_ref[...] = total[own:].astype(BF16)


def project_shapes(rows, own, width):
    parts = column_parts(width)
    columns = width // parts
    return [shaped((own, columns), F32)] * parts + [shaped((rows - own, columns), BF16)] * parts


def first_kernel(count, *refs):
    blocks, refs = refs[:count], refs[count:]
    flip_ref, table_ref, *qc_refs, qe_ref, gu_hbm = refs[:-8]
    hq_ref, mm_ref, *gu_refs = refs[-8:-4]
    tok_ref, rot_ref, mixed_ref, gu_sem = refs[-4:]
    units = hq_ref.shape[1]
    step = min(256, units)

    def full(k, block):
        cut = pl.ds(pl.multiple_of(block * step, step), step)
        return pltpu.make_async_copy(
            gu_hbm.at[k, :, cut], gu_refs[k].at[:, cut], gu_sem.at[k, block]
        )

    def full_arrived(block):
        for k in range(2):
            full(k, block).wait()

    for block in range(units // step):
        for k in range(2):
            full(k, block).start()
    sign = (1 - 2 * flip_ref[...]).astype(F32).astype(BF16)
    rotate_rows(blocks, sign, table_ref[...], tok_ref, mixed_ref, rot_ref)

    @pl.loop(0, units // step)
    def _(block):
        hidden_columns(
            block, step, tok_ref, rot_ref, gu_refs,
            lambda i, k, rows, cut: qc_refs[i * len(qc_refs) // 2 + k][:, cut],
            qe_ref, hq_ref, mm_ref, full_first=False, arrived=full_arrived,
        )


def first_hidden(blocks, flip, table, gate_up, codes, exps):
    rows, depth = len(blocks) * blocks[0].shape[0], blocks[0].shape[1]
    units = codes[0].shape[1]
    return pl.pallas_call(
        functools.partial(first_kernel, len(blocks)),
        in_specs=[spec(pltpu.VMEM)] * (len(blocks) + 3 + len(codes)) + [spec(pltpu.HBM)],
        out_specs=[spec(pltpu.VMEM)] * 4,
        out_shape=[
            shaped((rows, units), BF16),
            shaped((rows, units), BF16),
            pltpu.VMEM(gate_up.shape[1:], BF16),
            pltpu.VMEM(gate_up.shape[1:], BF16),
        ],
        scratch_shapes=[
            pltpu.VMEM((rows, depth), BF16),
            pltpu.VMEM((rows, depth), BF16),
            pltpu.VMEM((rows * depth // table.shape[0], table.shape[0]), F32),
            pltpu.SemaphoreType.DMA((2, units // min(256, units))),
        ],
        compiler_params=params(2 + (4 * rows * depth >> 19)),
        cost_estimate=pl.CostEstimate(
            flops=8 * rows * depth * units, transcendentals=0, bytes_accessed=2 * gate_up.size
        ),
        name="first_hidden",
    )(
        *blocks, flip, table, *codes, exps,
        pltpu.with_memory_space_constraint(gate_up, pltpu.HBM),
    )


def next_kernel(count, *refs):
    blocks, refs = refs[:count], refs[count:]
    flip_ref, table_ref, *gu_refs, qe_ref, down_ref, qc_hbm = refs[:7]
    hq_ref, *outs = refs[7:-6]
    tok_ref, rot_ref, mixed_ref, mm_ref, qc_ref, qc_sem = refs[-6:]
    units = hq_ref.shape[1]
    step = min(256, units)

    slots = qc_ref.shape[0]

    def codes(block):
        cut = pl.ds(pl.multiple_of(block * step, step), step)
        slot = lax.rem(block, slots)
        return pltpu.make_async_copy(qc_hbm.at[:, :, cut], qc_ref.at[slot], qc_sem.at[slot])

    for block in range(slots):
        codes(block).start()
    sign = (1 - 2 * flip_ref[...]).astype(F32).astype(BF16)
    rotate_rows(blocks, sign, table_ref[...], tok_ref, mixed_ref, rot_ref)

    @pl.loop(0, units // step)
    def _(block):
        slot = lax.rem(block, slots)
        hidden_columns(
            block, step, tok_ref, rot_ref, gu_refs,
            lambda i, k, rows, cut: qc_ref[slot, i, rows, :],
            qe_ref, hq_ref, mm_ref, full_first=True, arrived=lambda k: codes(k).wait(),
        )

        @pl.when(block + slots < units // step)
        def _():
            codes(block + slots).start()

    project(mm_ref, down_ref, outs[: len(outs) // 2], outs[len(outs) // 2 :])


def next_hidden(cores, blocks, flip, table, gate_up, codes, exps, down):
    rows, depth = len(blocks) * blocks[0].shape[0], blocks[0].shape[1]
    units, width = down.shape
    own = rows // cores
    step = min(256, units)
    slots = min(2, units // step)
    return pl.pallas_call(
        functools.partial(next_kernel, len(blocks)),
        in_specs=[spec(pltpu.VMEM)] * (len(blocks) + 6) + [spec(pltpu.HBM)],
        out_specs=[spec(pltpu.VMEM)] * (1 + 2 * column_parts(width)),
        out_shape=[shaped((rows, units), BF16)] + project_shapes(rows, own, width),
        scratch_shapes=[
            pltpu.VMEM((rows, depth), BF16),
            pltpu.VMEM((rows, depth), BF16),
            pltpu.VMEM((rows * depth // table.shape[0], table.shape[0]), F32),
            pltpu.VMEM((rows, units), BF16),
            pltpu.VMEM((slots, 2, depth, step), BF16),
            pltpu.SemaphoreType.DMA((slots,)),
        ],
        compiler_params=params(2 + (4 * rows * depth + 2 * slots * depth * step >> 19)),
        cost_estimate=pl.CostEstimate(
            flops=10 * rows * depth * units, transcendentals=0, bytes_accessed=2 * codes.size
        ),
        name="next_hidden",
    )(
        *blocks, flip, table, *gate_up, exps, down,
        pltpu.with_memory_space_constraint(codes, pltpu.HBM),
    )


def last_kernel(mm_ref, down_ref, *outs):
    project(mm_ref, down_ref, outs[: len(outs) // 2], outs[len(outs) // 2 :])


def last_project(cores, mm, down):
    rows, (units, width) = mm.shape[0], down.shape
    return pl.pallas_call(
        last_kernel,
        in_specs=[spec(pltpu.VMEM)] * 2,
        out_specs=[spec(pltpu.VMEM)] * (2 * column_parts(width)),
        out_shape=project_shapes(rows, rows // cores, width),
        compiler_params=params(4),
        name="last_project",
    )(mm, down)


def join_kernel(others, keep_ref, *refs):
    received, outs = refs[:others], refs[others:]
    rows = outs[0].shape[0]
    for k, out in enumerate(outs):
        cut = slice(k * rows, (k + 1) * rows)
        total = keep_ref[cut, :]
        for ref in received:
            total = total + ref[cut, :].astype(F32)
        out[...] = total.astype(BF16)


def join(lines, keep, received):
    rows = keep.shape[0] // lines
    block = shaped((rows, keep.shape[1]), BF16)
    return pl.pallas_call(
        functools.partial(join_kernel, len(received)),
        in_specs=[spec(pltpu.VMEM)] * (1 + len(received)),
        out_specs=[spec(pltpu.VMEM)] * lines,
        out_shape=[block] * lines,
        compiler_params=params(4),
        name="join",
    )(keep, *received)


def add_kernel(cut, whole, keep_ref, *refs):
    received, out = refs[:-1], refs[-1]
    total = keep_ref[cut, :]
    for k, ref in enumerate(received):
        total = total + (ref[cut, :] if k < whole else ref[...]).astype(F32)
    out[...] = total.astype(BF16)


def add(rows, line, keep, received, blocks):
    return pl.pallas_call(
        functools.partial(add_kernel, slice(line * rows, (line + 1) * rows), len(received)),
        in_specs=[spec(pltpu.VMEM)] * (1 + len(received) + len(blocks)),
        out_specs=spec(pltpu.VMEM),
        out_shape=shaped((rows, keep.shape[1]), BF16),
        compiler_params=params(4),
        name="add",
    )(keep, *received, *blocks)


def gram_kernel(scale, parts, part, *refs):
    hqs, blocks = refs[:parts], refs[parts : -6 - (part > 0)]
    o_hbm, hq_ref, turned_ref, proj_ref, o_ref, sem = refs[-6:]
    stack(hqs, hq_ref)
    stack(blocks, proj_ref)
    turned_ref[...] = hq_ref[...].T
    units, columns = o_ref.shape
    step = min(256, units)
    copies = []
    for k in range(units // step):
        cut = pl.ds(k * step, step)
        gram = jnp.dot(turned_ref[cut, :], proj_ref[...], preferred_element_type=F32)
        o_ref[cut, :] = (gram * scale).astype(BF16)
        target = o_hbm.at[cut, pl.ds(part * columns, columns)]
        copies.append(pltpu.make_async_copy(o_ref.at[cut], target, sem.at[k]))
        copies[-1].start()
    for copy in copies:
        copy.wait()


def gram(hqs, blocks, width, part, made):
    rows = sum(hq.shape[0] for hq in hqs)
    units, columns = hqs[0].shape[1], blocks[0].shape[1]
    count = len(hqs) + len(blocks)
    return pl.pallas_call(
        functools.partial(gram_kernel, 1.0 / rows**0.5, len(hqs), part),
        in_specs=[spec(pltpu.VMEM)] * count + [spec(pltpu.HBM)] * len(made),
        out_specs=spec(pltpu.HBM),
        out_shape=shaped((units, width), BF16),
        input_output_aliases={count: 0} if made else {},
        scratch_shapes=[
            pltpu.VMEM((rows, units), BF16),
            pltpu.VMEM((units, rows), BF16),
            pltpu.VMEM((rows, columns), BF16),
            pltpu.VMEM((units, columns), BF16),
            pltpu.SemaphoreType.DMA((units // min(256, units),)),
        ],
        compiler_params=params(20),
        name="gram",
    )(*hqs, *blocks, *made)


def grid_of(mesh):
    devices = mesh.devices.reshape(-1, mesh.shape["tok"])[0]
    spots = [tuple(d.coords) for d in devices]
    cores = sum(spot == spots[0] for spot in spots)
    chips = spots[::cores]
    side = next((k for k in range(1, len(chips)) if chips[k][2] != chips[0][2]), len(chips))
    if len(chips) % side:
        side = 1
    return len(chips) // side, side, cores


def shift(grid, axis, by):
    pairs = []
    for line in range(grid[0]):
        for side in range(grid[1]):
            for core in range(grid[2]):
                spot = [line, side, core]
                source = (spot[0] * grid[1] + spot[1]) * grid[2] + spot[2]
                spot[axis] = (spot[axis] + by) % grid[axis]
                pairs.append((source, (spot[0] * grid[1] + spot[1]) * grid[2] + spot[2]))
    return pairs


def far_first(lines):
    return sorted(range(lines), key=lambda s: -min(s, lines - s))


def gather(grid, block):
    send = lambda value, axis, by: lax.ppermute(value, "tok", shift(grid, axis, by))
    order = far_first(grid[0])[::-1]
    blocks = {}
    for line in order:
        blocks[0, 0, line] = send(block, 0, line) if line else block
    for by in range(grid[1]):
        for line in order:
            if by:
                blocks[by, 0, line] = send(blocks[0, 0, line], 1, by)
            for core in range(1, grid[2]):
                blocks[by, core, line] = send(blocks[by, 0, line], 2, core)
    return blocks, blocks[0, 0, order[1]]


def reduce_to_owner(grid, group, kept, sent):
    send = lambda value, axis, by: lax.ppermute(value, "tok", shift(grid, axis, -by))
    size = kept[0, 0].shape[0]
    rows = size // group
    received = {
        key: [send(sent[key][c * size :][:size], 2, c + 1) for c in range(grid[2] - 1)]
        for key in list(kept)[::-1]
    }
    moved = {line: [] for line in range(grid[0])}
    for by in range(grid[1] - 1, 0, -1):
        blocks = []
        for part in range(grid[0] // group):
            blocks += join(group, kept[by, part], received[by, part])
        for line in far_first(grid[0]):
            moved[line].append(send(blocks[line], 1, by))

    def total(line, arrived):
        key = 0, line // group
        return add(rows, line % group, kept[key], received[key], moved[line] + arrived)

    arrived = [send(total(line, []), 0, line) for line in far_first(grid[0])[:-1]]
    return total(0, arrived)


def solution(mesh):
    grid = grid_of(mesh)
    group = math.gcd(grid[0], 4)
    chunks = [(by, part) for by in range(grid[1]) for part in range(grid[0] // group)]

    def chunk_blocks(blocks, chunk):
        by, part = chunk
        lines = range(part * group, (part + 1) * group)
        return [blocks[by, core, line] for core in range(grid[2]) for line in lines]

    def per_device(tokens, rotation_flip, gate_up, quant_codes, quant_exps, down_rows):
        width = tokens.shape[1]
        held = lambda value: pltpu.with_memory_space_constraint(value, pltpu.VMEM)
        flip = rotation_flip.reshape(1, width)
        table = hadamard_table(min(256, width)).astype(BF16)
        blocks, near = gather(grid, tokens)
        codes = [held(value) for value in fetch(near, quant_codes, depth_pieces(quant_exps.shape[1]))]
        hq, mm, *gu = first_hidden(
            chunk_blocks(blocks, chunks[0]), flip, table, gate_up, codes, quant_exps
        )
        gu = [held(value) for value in gu]
        hqs, outs = [hq], {chunks[0]: None}
        for chunk in chunks[1:]:
            hq, *outs[chunk] = next_hidden(
                grid[2], chunk_blocks(blocks, chunk), flip, table, gu, quant_codes, quant_exps, down_rows
            )
            hqs.append(hq)
        outs[chunks[0]] = last_project(grid[2], mm, down_rows)
        out_width = down_rows.shape[1]
        parts = column_parts(out_width)
        owned, made = [], []
        for part in range(parts):
            kept = {chunk: outs[chunk][part] for chunk in chunks}
            sent = {chunk: outs[chunk][parts + part] for chunk in chunks}
            owned.append(reduce_to_owner(grid, group, kept, sent))
        for part, own in enumerate(owned):
            projected, _ = gather(grid, own)
            pieces = sum((chunk_blocks(projected, chunk) for chunk in chunks), [])
            made = [gram(hqs, pieces, out_width, part, made)]
        return made[0]

    placed = (
        P(("dom", "tok"), None),
        P(),
        P("dom", None, "tok"),
        P("dom", None, "tok"),
        P("dom", None, "tok"),
        P(("dom", "tok"), None),
    )
    return jax.shard_map(
        per_device, mesh=mesh, in_specs=placed, out_specs=P(("dom", "tok"), None), check_vma=False
    )
```

```python
import functools
import math

import jax
import jax.numpy as jnp
from jax import lax
from jax.experimental import pallas as pl
from jax.experimental.pallas import tpu as pltpu
from jax.sharding import PartitionSpec as P


F32 = jnp.float32
BF16 = jnp.bfloat16


def hadamard_table(order):
    index = jnp.arange(order, dtype=jnp.int32)
    common = index[:, None] & index[None, :]
    parity = jnp.zeros((order, order), jnp.int32)
    for bit_pos in range(max(order.bit_length() - 1, 1)):
        parity = parity ^ common >> bit_pos & 1
    return (1 - 2 * parity).astype(F32)


def spec(space):
    return pl.BlockSpec(memory_space=space)


def params(mib):
    return pltpu.CompilerParams(vmem_limit_bytes=mib << 20)


def shaped(dims, dtype):
    return jax.ShapeDtypeStruct(tuple(dims), dtype)


def stack(blocks, o_ref):
    rows = blocks[0].shape[0]
    for k, block in enumerate(blocks):
        o_ref[k * rows : (k + 1) * rows, :] = block[...]


def rotate_rows(blocks, sign, table, x_ref, mixed_ref, o_ref):
    stack(blocks, x_ref)
    rows, width = x_ref.shape
    inner = table.shape[0]
    count = width // inner
    scale = 1.0 / width**0.5
    signed = jnp.concatenate(
        [x_ref[:, k : k + inner] * sign[:, k : k + inner] for k in range(0, width, inner)], axis=0
    )
    mixed_ref[...] = jnp.dot(signed, table, preferred_element_type=F32)
    step = 16

    @pl.loop(0, rows // step)
    def _(block):
        row = pl.multiple_of(block * step, step)
        parts = [mixed_ref[pl.ds(k * rows + row, step), :] for k in range(count)]
        span = 1
        while span < count:
            for k in range(count):
                if not k & span:
                    a, b = parts[k], parts[k + span]
                    parts[k], parts[k + span] = a + b, a - b
            span *= 2
        for k, part in enumerate(parts):
            o_ref[pl.ds(row, step), k * inner : (k + 1) * inner] = (part * scale).astype(BF16)


def swiglu(pieces, input_ref, gate_of, upper_of):
    depth = input_ref.shape[1] // pieces
    gate = upper = 0.0
    for k in range(pieces):
        cut = slice(k * depth, (k + 1) * depth)
        inputs = input_ref[:, cut]
        gate = gate + jnp.dot(inputs, gate_of(k, cut), preferred_element_type=F32)
        upper = upper + jnp.dot(inputs, upper_of(k, cut), preferred_element_type=F32)
    return (gate / (1.0 + jnp.exp(-gate)) * upper).astype(BF16)


def depth_pieces(groups):
    return math.gcd(groups, 4)


def hidden_columns(
    block, width, tok_ref, rot_ref, gu_refs, codes_of, qe_ref, hq_ref, mm_ref, full_first, arrived
):
    depth = tok_ref.shape[1]
    groups = qe_ref.shape[1]
    pieces = depth_pieces(groups)
    cut = pl.ds(pl.multiple_of(block * width, width), width)

    def full_weight(i):
        return lambda k, rows: gu_refs[i][rows, cut]

    def quant_weight(i):
        def piece(k, rows):
            exps = qe_ref[i, k * groups // pieces : (k + 1) * groups // pieces, cut]
            scale = jnp.exp2(exps.astype(F32)).astype(BF16)
            codes = codes_of(i, k, rows, cut).reshape(groups // pieces, depth // groups, width)
            return (codes * scale[:, None, :]).reshape(depth // pieces, width)

        return piece

    if full_first:
        full = swiglu(pieces, tok_ref, full_weight(0), full_weight(1))
        arrived(block)
    quant = swiglu(pieces, rot_ref, quant_weight(0), quant_weight(1))
    if not full_first:
        arrived(block)
        full = swiglu(pieces, tok_ref, full_weight(0), full_weight(1))
    hq_ref[:, cut] = quant
    mm_ref[:, cut] = (full.astype(F32) - quant.astype(F32)).astype(BF16)


def fetch_kernel(_, source, *refs):
    targets, sem = refs[:-1], refs[-1]
    rows = targets[0].shape[0]
    pieces = source.shape[1] // rows
    copies = [
        pltpu.make_async_copy(
            source.at[k // pieces, pl.ds(k % pieces * rows, rows)], target, sem.at[k]
        )
        for k, target in enumerate(targets)
    ]
    for copy in copies:
        copy.start()
    for copy in copies:
        copy.wait()


def fetch(after, weights, pieces):
    count = weights.shape[0] * pieces
    dims = weights.shape[1] // pieces, weights.shape[2]
    return pl.pallas_call(
        fetch_kernel,
        in_specs=[spec(pltpu.VMEM), spec(pltpu.HBM)],
        out_specs=[spec(pltpu.VMEM)] * count,
        out_shape=[pltpu.VMEM(dims, weights.dtype)] * count,
        scratch_shapes=[pltpu.SemaphoreType.DMA((count,))],
        compiler_params=params(1),
        cost_estimate=pl.CostEstimate(
            flops=0, transcendentals=0, bytes_accessed=4 * weights.size
        ),
        name="fetch",
    )(after, pltpu.with_memory_space_constraint(weights, pltpu.HBM))


def project(mm_ref, down_ref, keep_ref, send_ref):
    total = jnp.dot(mm_ref[...], down_ref[...], preferred_element_type=F32)
    own = keep_ref.shape[0]
    keep_ref[...] = total[:own]
    send_ref[...] = total[own:].astype(BF16)


def project_shapes(rows, own, width):
    return [shaped((own, width), F32), shaped((rows - own, width), BF16)]


def first_kernel(count, *refs):
    blocks, refs = refs[:count], refs[count:]
    flip_ref, table_ref, *qc_refs, qe_ref, gu_hbm = refs[:-8]
    hq_ref, mm_ref, *gu_refs = refs[-8:-4]
    tok_ref, rot_ref, mixed_ref, gu_sem = refs[-4:]
    units = hq_ref.shape[1]
    step = min(256, units)

    def full(k, block):
        cut = pl.ds(pl.multiple_of(block * step, step), step)
        return pltpu.make_async_copy(
            gu_hbm.at[k, :, cut], gu_refs[k].at[:, cut], gu_sem.at[k, block]
        )

    def full_arrived(block):
        for k in range(2):
            full(k, block).wait()

    for block in range(units // step):
        for k in range(2):
            full(k, block).start()
    sign = (1 - 2 * flip_ref[...]).astype(F32).astype(BF16)
    rotate_rows(blocks, sign, table_ref[...], tok_ref, mixed_ref, rot_ref)

    @pl.loop(0, units // step)
    def _(block):
        hidden_columns(
            block, step, tok_ref, rot_ref, gu_refs,
            lambda i, k, rows, cut: qc_refs[i * len(qc_refs) // 2 + k][:, cut],
            qe_ref, hq_ref, mm_ref, full_first=False, arrived=full_arrived,
        )


def first_hidden(blocks, flip, table, gate_up, codes, exps):
    rows, depth = len(blocks) * blocks[0].shape[0], blocks[0].shape[1]
    units = codes[0].shape[1]
    return pl.pallas_call(
        functools.partial(first_kernel, len(blocks)),
        in_specs=[spec(pltpu.VMEM)] * (len(blocks) + 3 + len(codes)) + [spec(pltpu.HBM)],
        out_specs=[spec(pltpu.VMEM)] * 4,
        out_shape=[
            shaped((rows, units), BF16),
            shaped((rows, units), BF16),
            pltpu.VMEM(gate_up.shape[1:], BF16),
            pltpu.VMEM(gate_up.shape[1:], BF16),
        ],
        scratch_shapes=[
            pltpu.VMEM((rows, depth), BF16),
            pltpu.VMEM((rows, depth), BF16),
            pltpu.VMEM((rows * depth // table.shape[0], table.shape[0]), F32),
            pltpu.SemaphoreType.DMA((2, units // min(256, units))),
        ],
        compiler_params=params(2 + (4 * rows * depth >> 19)),
        cost_estimate=pl.CostEstimate(
            flops=8 * rows * depth * units, transcendentals=0, bytes_accessed=2 * gate_up.size
        ),
        name="first_hidden",
    )(
        *blocks, flip, table, *codes, exps,
        pltpu.with_memory_space_constraint(gate_up, pltpu.HBM),
    )


def next_kernel(count, *refs):
    blocks, refs = refs[:count], refs[count:]
    flip_ref, table_ref, *gu_refs, qe_ref, down_ref, qc_hbm = refs[:7]
    hq_ref, *outs = refs[7:-6]
    tok_ref, rot_ref, mixed_ref, mm_ref, qc_ref, qc_sem = refs[-6:]
    units = hq_ref.shape[1]
    step = min(256, units)

    slots = qc_ref.shape[0]

    def codes(block):
        cut = pl.ds(pl.multiple_of(block * step, step), step)
        slot = lax.rem(block, slots)
        return pltpu.make_async_copy(qc_hbm.at[:, :, cut], qc_ref.at[slot], qc_sem.at[slot])

    for block in range(slots):
        codes(block).start()
    sign = (1 - 2 * flip_ref[...]).astype(F32).astype(BF16)
    rotate_rows(blocks, sign, table_ref[...], tok_ref, mixed_ref, rot_ref)

    @pl.loop(0, units // step)
    def _(block):
        slot = lax.rem(block, slots)
        hidden_columns(
            block, step, tok_ref, rot_ref, gu_refs,
            lambda i, k, rows, cut: qc_ref[slot, i, rows, :],
            qe_ref, hq_ref, mm_ref, full_first=True, arrived=lambda k: codes(k).wait(),
        )

        @pl.when(block + slots < units // step)
        def _():
            codes(block + slots).start()

    project(mm_ref, down_ref, *outs)


def next_hidden(cores, blocks, flip, table, gate_up, codes, exps, down):
    rows, depth = len(blocks) * blocks[0].shape[0], blocks[0].shape[1]
    units, width = down.shape
    own = rows // cores
    step = min(256, units)
    slots = min(2, units // step)
    return pl.pallas_call(
        functools.partial(next_kernel, len(blocks)),
        in_specs=[spec(pltpu.VMEM)] * (len(blocks) + 6) + [spec(pltpu.HBM)],
        out_specs=[spec(pltpu.VMEM)] * 3,
        out_shape=[shaped((rows, units), BF16)] + project_shapes(rows, own, width),
        scratch_shapes=[
            pltpu.VMEM((rows, depth), BF16),
            pltpu.VMEM((rows, depth), BF16),
            pltpu.VMEM((rows * depth // table.shape[0], table.shape[0]), F32),
            pltpu.VMEM((rows, units), BF16),
            pltpu.VMEM((slots, 2, depth, step), BF16),
            pltpu.SemaphoreType.DMA((slots,)),
        ],
        compiler_params=params(2 + (4 * rows * depth + 2 * slots * depth * step >> 19)),
        cost_estimate=pl.CostEstimate(
            flops=10 * rows * depth * units, transcendentals=0, bytes_accessed=2 * codes.size
        ),
        name="next_hidden",
    )(
        *blocks, flip, table, *gate_up, exps, down,
        pltpu.with_memory_space_constraint(codes, pltpu.HBM),
    )


def last_kernel(mm_ref, down_ref, *outs):
    project(mm_ref, down_ref, *outs)


def last_project(cores, mm, down):
    rows, (units, width) = mm.shape[0], down.shape
    return pl.pallas_call(
        last_kernel,
        in_specs=[spec(pltpu.VMEM)] * 2,
        out_specs=[spec(pltpu.VMEM)] * 2,
        out_shape=project_shapes(rows, rows // cores, width),
        compiler_params=params(4),
        name="last_project",
    )(mm, down)


def join_kernel(others, keep_ref, *refs):
    received, outs = refs[:others], refs[others:]
    rows = outs[0].shape[0]
    for k, out in enumerate(outs):
        cut = slice(k * rows, (k + 1) * rows)
        total = keep_ref[cut, :]
        for ref in received:
            total = total + ref[cut, :].astype(F32)
        out[...] = total.astype(BF16)


def join(lines, keep, received):
    rows = keep.shape[0] // lines
    block = shaped((rows, keep.shape[1]), BF16)
    return pl.pallas_call(
        functools.partial(join_kernel, len(received)),
        in_specs=[spec(pltpu.VMEM)] * (1 + len(received)),
        out_specs=[spec(pltpu.VMEM)] * lines,
        out_shape=[block] * lines,
        compiler_params=params(4),
        name="join",
    )(keep, *received)


def add_kernel(cut, whole, keep_ref, *refs):
    received, out = refs[:-1], refs[-1]
    total = keep_ref[cut, :]
    for k, ref in enumerate(received):
        total = total + (ref[cut, :] if k < whole else ref[...]).astype(F32)
    out[...] = total.astype(BF16)


def add(rows, line, keep, received, blocks):
    return pl.pallas_call(
        functools.partial(add_kernel, slice(line * rows, (line + 1) * rows), len(received)),
        in_specs=[spec(pltpu.VMEM)] * (1 + len(received) + len(blocks)),
        out_specs=spec(pltpu.VMEM),
        out_shape=shaped((rows, keep.shape[1]), BF16),
        compiler_params=params(4),
        name="add",
    )(keep, *received, *blocks)


def turn_kernel(parts, *refs):
    o_ref, hq_ref = refs[-2:]
    stack(refs[:parts], hq_ref)
    o_ref[...] = hq_ref[...].T


def turn(hqs):
    rows, units = sum(hq.shape[0] for hq in hqs), hqs[0].shape[1]
    return pl.pallas_call(
        functools.partial(turn_kernel, len(hqs)),
        in_specs=[spec(pltpu.VMEM)] * len(hqs),
        out_specs=spec(pltpu.VMEM),
        out_shape=shaped((units, rows), BF16),
        scratch_shapes=[pltpu.VMEM((rows, units), BF16)],
        compiler_params=params(4),
        name="turn",
    )(*hqs)


def gram_kernel(scale, turned_ref, *refs):
    blocks, (o_hbm, proj_ref, o_ref, sem) = refs[:-4], refs[-4:]
    stack(blocks, proj_ref)
    units = turned_ref.shape[0]
    step = min(128, units)
    copies = []
    for k in range(units // step):
        cut = pl.ds(k * step, step)
        gram = jnp.dot(turned_ref[cut, :], proj_ref[...], preferred_element_type=F32)
        o_ref[cut, :] = (gram * scale).astype(BF16)
        copies.append(pltpu.make_async_copy(o_ref.at[cut], o_hbm.at[cut], sem.at[k]))
        copies[-1].start()
    for copy in copies:
        copy.wait()


def gram(turned, blocks):
    units, rows = turned.shape
    out = blocks[0].shape[1]
    return pl.pallas_call(
        functools.partial(gram_kernel, 1.0 / rows**0.5),
        in_specs=[spec(pltpu.VMEM)] * (1 + len(blocks)),
        out_specs=spec(pltpu.HBM),
        out_shape=shaped((units, out), BF16),
        scratch_shapes=[
            pltpu.VMEM((rows, out), BF16),
            pltpu.VMEM((units, out), BF16),
            pltpu.SemaphoreType.DMA((units // min(128, units),)),
        ],
        compiler_params=params(24),
        name="gram",
    )(turned, *blocks)


def grid_of(mesh):
    devices = mesh.devices.reshape(-1, mesh.shape["tok"])[0]
    spots = [tuple(d.coords) for d in devices]
    cores = sum(spot == spots[0] for spot in spots)
    chips = spots[::cores]
    side = next((k for k in range(1, len(chips)) if chips[k][2] != chips[0][2]), len(chips))
    if len(chips) % side:
        side = 1
    return len(chips) // side, side, cores


def mirrored(length):
    return length & (length - 1) == 0


def shift(grid, axis, by):
    pairs = []
    for line in range(grid[0]):
        for side in range(grid[1]):
            for core in range(grid[2]):
                spot = [line, side, core]
                source = (spot[0] * grid[1] + spot[1]) * grid[2] + spot[2]
                if mirrored(grid[axis]):
                    spot[axis] ^= abs(by)
                else:
                    spot[axis] = (spot[axis] + by) % grid[axis]
                pairs.append((source, (spot[0] * grid[1] + spot[1]) * grid[2] + spot[2]))
    return pairs


def far_first(lines):
    if mirrored(lines):
        return list(range(lines))[::-1]
    return sorted(range(lines), key=lambda s: -min(s, lines - s))


def gather(grid, block):
    send = lambda value, axis, by: lax.ppermute(value, "tok", shift(grid, axis, by))
    order = far_first(grid[0])[::-1]
    blocks = {}
    for line in order:
        blocks[0, 0, line] = send(block, 0, line) if line else block
    for by in range(grid[1]):
        for line in order:
            if by:
                blocks[by, 0, line] = send(blocks[0, 0, line], 1, by)
            for core in range(1, grid[2]):
                blocks[by, core, line] = send(blocks[by, 0, line], 2, core)
    return blocks, blocks[0, 0, order[1]]


def reduce_to_owner(grid, group, kept, sent):
    send = lambda value, axis, by: lax.ppermute(value, "tok", shift(grid, axis, -by))
    size = kept[0, 0].shape[0]
    rows = size // group
    received = {
        key: [send(sent[key][c * size :][:size], 2, c + 1) for c in range(grid[2] - 1)]
        for key in list(kept)[::-1]
    }
    moved = {line: [] for line in range(grid[0])}
    for by in range(grid[1] - 1, 0, -1):
        blocks = []
        for part in range(grid[0] // group):
            blocks += join(group, kept[by, part], received[by, part])
        for line in far_first(grid[0]):
            moved[line].append(send(blocks[line], 1, by))

    def total(line, arrived):
        key = 0, line // group
        return add(rows, line % group, kept[key], received[key], moved[line] + arrived)

    arrived = [send(total(line, []), 0, line) for line in far_first(grid[0])[:-1]]
    return total(0, arrived)


def solution(mesh):
    grid = grid_of(mesh)
    group = math.gcd(grid[0], 4)
    chunks = [(by, part) for by in range(grid[1]) for part in range(grid[0] // group)]

    def chunk_blocks(blocks, chunk):
        by, part = chunk
        lines = range(part * group, (part + 1) * group)
        return [blocks[by, core, line] for core in range(grid[2]) for line in lines]

    def per_device(tokens, rotation_flip, gate_up, quant_codes, quant_exps, down_rows):
        width = tokens.shape[1]
        held = lambda value: pltpu.with_memory_space_constraint(value, pltpu.VMEM)
        flip = rotation_flip.reshape(1, width)
        table = hadamard_table(min(256, width)).astype(BF16)
        blocks, near = gather(grid, tokens)
        codes = [held(value) for value in fetch(near, quant_codes, depth_pieces(quant_exps.shape[1]))]
        hq, mm, *gu = first_hidden(
            chunk_blocks(blocks, chunks[0]), flip, table, gate_up, codes, quant_exps
        )
        gu = [held(value) for value in gu]
        hqs, outs = [hq], {chunks[0]: None}
        for chunk in chunks[1:]:
            hq, *outs[chunk] = next_hidden(
                grid[2], chunk_blocks(blocks, chunk), flip, table, gu, quant_codes, quant_exps, down_rows
            )
            hqs.append(hq)
        outs[chunks[0]] = last_project(grid[2], mm, down_rows)
        kept = {chunk: outs[chunk][0] for chunk in chunks}
        sent = {chunk: outs[chunk][1] for chunk in chunks}
        own = reduce_to_owner(grid, group, kept, sent)
        turned = turn(hqs)
        projected, _ = gather(grid, own)
        return gram(turned, sum((chunk_blocks(projected, chunk) for chunk in chunks), []))

    placed = (
        P(("dom", "tok"), None),
        P(),
        P("dom", None, "tok"),
        P("dom", None, "tok"),
        P("dom", None, "tok"),
        P(("dom", "tok"), None),
    )
    return jax.shard_map(
        per_device, mesh=mesh, in_specs=placed, out_specs=P(("dom", "tok"), None), check_vma=False
    )
```

```python
import functools
import math

import jax
import jax.numpy as jnp
from jax import lax
from jax.experimental import pallas as pl
from jax.experimental.pallas import tpu as pltpu
from jax.sharding import PartitionSpec as P


F32 = jnp.float32
BF16 = jnp.bfloat16


def hadamard_table(order):
    index = jnp.arange(order, dtype=jnp.int32)
    common = index[:, None] & index[None, :]
    parity = jnp.zeros((order, order), jnp.int32)
    for bit_pos in range(max(order.bit_length() - 1, 1)):
        parity = parity ^ common >> bit_pos & 1
    return (1 - 2 * parity).astype(F32)


def spec(space):
    return pl.BlockSpec(memory_space=space)


def params(mib):
    return pltpu.CompilerParams(vmem_limit_bytes=mib << 20)


def shaped(dims, dtype):
    return jax.ShapeDtypeStruct(tuple(dims), dtype)


def stack(blocks, o_ref):
    rows = blocks[0].shape[0]
    for k, block in enumerate(blocks):
        o_ref[k * rows : (k + 1) * rows, :] = block[...]


def rotate_rows(blocks, sign, table, x_ref, mixed_ref, o_ref):
    stack(blocks, x_ref)
    rows, width = x_ref.shape
    inner = table.shape[0]
    count = width // inner
    scale = 1.0 / width**0.5
    signed = jnp.concatenate(
        [x_ref[:, k : k + inner] * sign[:, k : k + inner] for k in range(0, width, inner)], axis=0
    )
    mixed_ref[...] = jnp.dot(signed, table, preferred_element_type=F32)
    step = 16

    @pl.loop(0, rows // step)
    def _(block):
        row = pl.multiple_of(block * step, step)
        parts = [mixed_ref[pl.ds(k * rows + row, step), :] for k in range(count)]
        span = 1
        while span < count:
            for k in range(count):
                if not k & span:
                    a, b = parts[k], parts[k + span]
                    parts[k], parts[k + span] = a + b, a - b
            span *= 2
        for k, part in enumerate(parts):
            o_ref[pl.ds(row, step), k * inner : (k + 1) * inner] = (part * scale).astype(BF16)


def swiglu(pieces, input_ref, gate_of, upper_of):
    depth = input_ref.shape[1] // pieces
    gate = upper = 0.0
    for k in range(pieces):
        cut = slice(k * depth, (k + 1) * depth)
        inputs = input_ref[:, cut]
        gate = gate + jnp.dot(inputs, gate_of(k, cut), preferred_element_type=F32)
        upper = upper + jnp.dot(inputs, upper_of(k, cut), preferred_element_type=F32)
    return (gate / (1.0 + jnp.exp(-gate)) * upper).astype(BF16)


def depth_pieces(groups):
    return math.gcd(groups, 4)


def hidden_columns(
    block, width, tok_ref, rot_ref, gu_refs, codes_of, qe_ref, hq_ref, mm_ref, only, arrived
):
    depth = tok_ref.shape[1]
    groups = qe_ref.shape[1]
    pieces = depth_pieces(groups)
    cut = pl.ds(pl.multiple_of(block * width, width), width)

    def full_weight(i):
        return lambda k, rows: gu_refs[i][rows, cut]

    def quant_weight(i):
        def piece(k, rows):
            exps = qe_ref[i, k * groups // pieces : (k + 1) * groups // pieces, cut]
            scale = jnp.exp2(exps.astype(F32)).astype(BF16)
            codes = codes_of(i, k, rows, cut).reshape(groups // pieces, depth // groups, width)
            return (codes * scale[:, None, :]).reshape(depth // pieces, width)

        return piece

    if only != "quant":
        if only:
            arrived(block)
        full = swiglu(pieces, tok_ref, full_weight(0), full_weight(1))
    if only == "full":
        quant = hq_ref[:, cut]
    else:
        if not only:
            arrived(block)
        quant = swiglu(pieces, rot_ref, quant_weight(0), quant_weight(1))
        hq_ref[:, cut] = quant
    if only == "quant":
        return
    mm_ref[:, cut] = (full.astype(F32) - quant.astype(F32)).astype(BF16)


def fetch_kernel(_, source, *refs):
    targets, sem = refs[:-1], refs[-1]
    rows = targets[0].shape[0]
    pieces = source.shape[1] // rows
    copies = [
        pltpu.make_async_copy(
            source.at[k // pieces, pl.ds(k % pieces * rows, rows)], target, sem.at[k]
        )
        for k, target in enumerate(targets)
    ]
    for copy in copies:
        copy.start()
    for copy in copies:
        copy.wait()


def fetch(after, weights, pieces):
    count = weights.shape[0] * pieces
    dims = weights.shape[1] // pieces, weights.shape[2]
    return pl.pallas_call(
        fetch_kernel,
        in_specs=[spec(pltpu.VMEM), spec(pltpu.HBM)],
        out_specs=[spec(pltpu.VMEM)] * count,
        out_shape=[pltpu.VMEM(dims, weights.dtype)] * count,
        scratch_shapes=[pltpu.SemaphoreType.DMA((count,))],
        compiler_params=params(1),
        cost_estimate=pl.CostEstimate(
            flops=0, transcendentals=0, bytes_accessed=4 * weights.size
        ),
        name="fetch",
    )(after, pltpu.with_memory_space_constraint(weights, pltpu.HBM))


def project(mm_ref, down_ref, keep_ref, send_ref):
    total = jnp.dot(mm_ref[...], down_ref[...], preferred_element_type=F32)
    own = keep_ref.shape[0]
    keep_ref[...] = total[:own]
    send_ref[...] = total[own:].astype(BF16)


def project_shapes(rows, own, width):
    return [shaped((own, width), F32), shaped((rows - own, width), BF16)]


def first_kernel(count, *refs):
    blocks, refs = refs[:count], refs[count:]
    flip_ref, table_ref, *qc_refs, qe_ref, gu_hbm = refs[:-8]
    hq_ref, mm_ref, *gu_refs = refs[-8:-4]
    tok_ref, rot_ref, mixed_ref, gu_sem = refs[-4:]
    units = hq_ref.shape[1]
    step = min(256, units)

    def full(k, block):
        cut = pl.ds(pl.multiple_of(block * step, step), step)
        return pltpu.make_async_copy(
            gu_hbm.at[k, :, cut], gu_refs[k].at[:, cut], gu_sem.at[k, block]
        )

    def full_arrived(block):
        for k in range(2):
            full(k, block).wait()

    for block in range(units // step):
        for k in range(2):
            full(k, block).start()
    sign = (1 - 2 * flip_ref[...]).astype(F32).astype(BF16)
    rotate_rows(blocks, sign, table_ref[...], tok_ref, mixed_ref, rot_ref)

    for only in ("quant", "full"):

        @pl.loop(0, units // step)
        def _(block):
            hidden_columns(
                block, step, tok_ref, rot_ref, gu_refs,
                lambda i, k, rows, cut: qc_refs[i * len(qc_refs) // 2 + k][:, cut],
                qe_ref, hq_ref, mm_ref, only=only, arrived=full_arrived,
            )


def first_hidden(blocks, flip, table, gate_up, codes, exps):
    rows, depth = len(blocks) * blocks[0].shape[0], blocks[0].shape[1]
    units = codes[0].shape[1]
    return pl.pallas_call(
        functools.partial(first_kernel, len(blocks)),
        in_specs=[spec(pltpu.VMEM)] * (len(blocks) + 3 + len(codes)) + [spec(pltpu.HBM)],
        out_specs=[spec(pltpu.VMEM)] * 4,
        out_shape=[
            shaped((rows, units), BF16),
            shaped((rows, units), BF16),
            pltpu.VMEM(gate_up.shape[1:], BF16),
            pltpu.VMEM(gate_up.shape[1:], BF16),
        ],
        scratch_shapes=[
            pltpu.VMEM((rows, depth), BF16),
            pltpu.VMEM((rows, depth), BF16),
            pltpu.VMEM((rows * depth // table.shape[0], table.shape[0]), F32),
            pltpu.SemaphoreType.DMA((2, units // min(256, units))),
        ],
        compiler_params=params(2 + (4 * rows * depth >> 19)),
        cost_estimate=pl.CostEstimate(
            flops=8 * rows * depth * units, transcendentals=0, bytes_accessed=2 * gate_up.size
        ),
        name="first_hidden",
    )(
        *blocks, flip, table, *codes, exps,
        pltpu.with_memory_space_constraint(gate_up, pltpu.HBM),
    )


def next_kernel(count, *refs):
    blocks, refs = refs[:count], refs[count:]
    flip_ref, table_ref, *gu_refs, qe_ref, down_ref, qc_hbm = refs[:7]
    hq_ref, *outs = refs[7:-6]
    tok_ref, rot_ref, mixed_ref, mm_ref, qc_ref, qc_sem = refs[-6:]
    units = hq_ref.shape[1]
    step = min(256, units)

    slots = qc_ref.shape[0]

    def codes(block):
        cut = pl.ds(pl.multiple_of(block * step, step), step)
        slot = lax.rem(block, slots)
        return pltpu.make_async_copy(qc_hbm.at[:, :, cut], qc_ref.at[slot], qc_sem.at[slot])

    codes(0).start()
    sign = (1 - 2 * flip_ref[...]).astype(F32).astype(BF16)
    rotate_rows(blocks, sign, table_ref[...], tok_ref, mixed_ref, rot_ref)
    for block in range(1, slots):
        codes(block).start()

    @pl.loop(0, units // step)
    def _(block):
        slot = lax.rem(block, slots)
        hidden_columns(
            block, step, tok_ref, rot_ref, gu_refs,
            lambda i, k, rows, cut: qc_ref[slot, i, rows, :],
            qe_ref, hq_ref, mm_ref, only=None, arrived=lambda k: codes(k).wait(),
        )

        @pl.when(block + slots < units // step)
        def _():
            codes(block + slots).start()

    project(mm_ref, down_ref, *outs)


def next_hidden(cores, blocks, flip, table, gate_up, codes, exps, down):
    rows, depth = len(blocks) * blocks[0].shape[0], blocks[0].shape[1]
    units, width = down.shape
    own = rows // cores
    step = min(256, units)
    slots = min(2, units // step)
    return pl.pallas_call(
        functools.partial(next_kernel, len(blocks)),
        in_specs=[spec(pltpu.VMEM)] * (len(blocks) + 6) + [spec(pltpu.HBM)],
        out_specs=[spec(pltpu.VMEM)] * 3,
        out_shape=[shaped((rows, units), BF16)] + project_shapes(rows, own, width),
        scratch_shapes=[
            pltpu.VMEM((rows, depth), BF16),
            pltpu.VMEM((rows, depth), BF16),
            pltpu.VMEM((rows * depth // table.shape[0], table.shape[0]), F32),
            pltpu.VMEM((rows, units), BF16),
            pltpu.VMEM((slots, 2, depth, step), BF16),
            pltpu.SemaphoreType.DMA((slots,)),
        ],
        compiler_params=params(2 + (4 * rows * depth + 2 * slots * depth * step >> 19)),
        cost_estimate=pl.CostEstimate(
            flops=10 * rows * depth * units, transcendentals=0, bytes_accessed=2 * codes.size
        ),
        name="next_hidden",
    )(
        *blocks, flip, table, *gate_up, exps, down,
        pltpu.with_memory_space_constraint(codes, pltpu.HBM),
    )


def last_kernel(mm_ref, down_ref, *outs):
    project(mm_ref, down_ref, *outs)


def last_project(cores, mm, down):
    rows, (units, width) = mm.shape[0], down.shape
    return pl.pallas_call(
        last_kernel,
        in_specs=[spec(pltpu.VMEM)] * 2,
        out_specs=[spec(pltpu.VMEM)] * 2,
        out_shape=project_shapes(rows, rows // cores, width),
        compiler_params=params(4),
        name="last_project",
    )(mm, down)


def join_kernel(others, keep_ref, *refs):
    received, outs = refs[:others], refs[others:]
    rows = outs[0].shape[0]
    for k, out in enumerate(outs):
        cut = slice(k * rows, (k + 1) * rows)
        total = keep_ref[cut, :]
        for ref in received:
            total = total + ref[cut, :].astype(F32)
        out[...] = total.astype(BF16)


def join(lines, keep, received):
    rows = keep.shape[0] // lines
    block = shaped((rows, keep.shape[1]), BF16)
    return pl.pallas_call(
        functools.partial(join_kernel, len(received)),
        in_specs=[spec(pltpu.VMEM)] * (1 + len(received)),
        out_specs=[spec(pltpu.VMEM)] * lines,
        out_shape=[block] * lines,
        compiler_params=params(4),
        name="join",
    )(keep, *received)


def add_kernel(cut, whole, keep_ref, *refs):
    received, out = refs[:-1], refs[-1]
    total = keep_ref[cut, :]
    for k, ref in enumerate(received):
        total = total + (ref[cut, :] if k < whole else ref[...]).astype(F32)
    out[...] = total.astype(BF16)


def add(rows, line, keep, received, blocks):
    return pl.pallas_call(
        functools.partial(add_kernel, slice(line * rows, (line + 1) * rows), len(received)),
        in_specs=[spec(pltpu.VMEM)] * (1 + len(received) + len(blocks)),
        out_specs=spec(pltpu.VMEM),
        out_shape=shaped((rows, keep.shape[1]), BF16),
        compiler_params=params(4),
        name="add",
    )(keep, *received, *blocks)


def turn_kernel(parts, *refs):
    o_ref, hq_ref = refs[-2:]
    stack(refs[:parts], hq_ref)
    o_ref[...] = hq_ref[...].T


def turn(hqs):
    rows, units = sum(hq.shape[0] for hq in hqs), hqs[0].shape[1]
    return pl.pallas_call(
        functools.partial(turn_kernel, len(hqs)),
        in_specs=[spec(pltpu.VMEM)] * len(hqs),
        out_specs=spec(pltpu.VMEM),
        out_shape=shaped((units, rows), BF16),
        scratch_shapes=[pltpu.VMEM((rows, units), BF16)],
        compiler_params=params(4),
        name="turn",
    )(*hqs)


def gram_kernel(scale, turned_ref, *refs):
    blocks, (o_hbm, proj_ref, o_ref, sem) = refs[:-4], refs[-4:]
    stack(blocks, proj_ref)
    units = turned_ref.shape[0]
    step = min(128, units)
    copies = []
    for k in range(units // step):
        cut = pl.ds(k * step, step)
        gram = jnp.dot(turned_ref[cut, :], proj_ref[...], preferred_element_type=F32)
        o_ref[cut, :] = (gram * scale).astype(BF16)
        copies.append(pltpu.make_async_copy(o_ref.at[cut], o_hbm.at[cut], sem.at[k]))
        copies[-1].start()
    for copy in copies:
        copy.wait()


def gram(turned, blocks):
    units, rows = turned.shape
    out = blocks[0].shape[1]
    return pl.pallas_call(
        functools.partial(gram_kernel, 1.0 / rows**0.5),
        in_specs=[spec(pltpu.VMEM)] * (1 + len(blocks)),
        out_specs=spec(pltpu.HBM),
        out_shape=shaped((units, out), BF16),
        scratch_shapes=[
            pltpu.VMEM((rows, out), BF16),
            pltpu.VMEM((units, out), BF16),
            pltpu.SemaphoreType.DMA((units // min(128, units),)),
        ],
        compiler_params=params(24),
        name="gram",
    )(turned, *blocks)


def grid_of(mesh):
    devices = mesh.devices.reshape(-1, mesh.shape["tok"])[0]
    spots = [tuple(d.coords) for d in devices]
    cores = sum(spot == spots[0] for spot in spots)
    chips = spots[::cores]
    side = next((k for k in range(1, len(chips)) if chips[k][2] != chips[0][2]), len(chips))
    if len(chips) % side:
        side = 1
    return len(chips) // side, side, cores


def mirrored(length):
    return length & (length - 1) == 0


def shift(grid, axis, by):
    pairs = []
    for line in range(grid[0]):
        for side in range(grid[1]):
            for core in range(grid[2]):
                spot = [line, side, core]
                source = (spot[0] * grid[1] + spot[1]) * grid[2] + spot[2]
                if mirrored(grid[axis]):
                    spot[axis] ^= abs(by)
                else:
                    spot[axis] = (spot[axis] + by) % grid[axis]
                pairs.append((source, (spot[0] * grid[1] + spot[1]) * grid[2] + spot[2]))
    return pairs


def far_first(lines):
    if mirrored(lines):
        return list(range(lines))[::-1]
    return sorted(range(lines), key=lambda s: -min(s, lines - s))


def gather(grid, block):
    send = lambda value, axis, by: lax.ppermute(value, "tok", shift(grid, axis, by))
    order = far_first(grid[0])[::-1]
    blocks = {}
    for line in order:
        blocks[0, 0, line] = send(block, 0, line) if line else block
    for by in range(grid[1]):
        for line in order:
            if by:
                blocks[by, 0, line] = send(blocks[0, 0, line], 1, by)
            for core in range(1, grid[2]):
                blocks[by, core, line] = send(blocks[by, 0, line], 2, core)
    return blocks, blocks[0, 0, order[1]]


def reduce_to_owner(grid, group, kept, sent):
    send = lambda value, axis, by: lax.ppermute(value, "tok", shift(grid, axis, -by))
    size = kept[0, 0].shape[0]
    rows = size // group
    received = {
        key: [send(sent[key][c * size :][:size], 2, c + 1) for c in range(grid[2] - 1)]
        for key in list(kept)[::-1]
    }
    moved = {line: [] for line in range(grid[0])}
    for by in range(grid[1] - 1, 0, -1):
        blocks = []
        for part in range(grid[0] // group):
            blocks += join(group, kept[by, part], received[by, part])
        for line in far_first(grid[0]):
            moved[line].append(send(blocks[line], 1, by))

    def total(line, arrived):
        key = 0, line // group
        return add(rows, line % group, kept[key], received[key], moved[line] + arrived)

    arrived = [send(total(line, []), 0, line) for line in far_first(grid[0])[:-1]]
    return total(0, arrived)


def solution(mesh):
    grid = grid_of(mesh)
    group = math.gcd(grid[0], 4)
    chunks = [(by, part) for by in range(grid[1]) for part in range(grid[0] // group)]

    def chunk_blocks(blocks, chunk):
        by, part = chunk
        lines = range(part * group, (part + 1) * group)
        return [blocks[by, core, line] for core in range(grid[2]) for line in lines]

    def per_device(tokens, rotation_flip, gate_up, quant_codes, quant_exps, down_rows):
        width = tokens.shape[1]
        held = lambda value: pltpu.with_memory_space_constraint(value, pltpu.VMEM)
        flip = rotation_flip.reshape(1, width)
        table = hadamard_table(min(256, width)).astype(BF16)
        blocks, near = gather(grid, tokens)
        codes = [held(value) for value in fetch(near, quant_codes, depth_pieces(quant_exps.shape[1]))]
        hq, mm, *gu = first_hidden(
            chunk_blocks(blocks, chunks[0]), flip, table, gate_up, codes, quant_exps
        )
        gu = [held(value) for value in gu]
        hqs, outs = [hq], {chunks[0]: None}
        for chunk in chunks[1:]:
            hq, *outs[chunk] = next_hidden(
                grid[2], chunk_blocks(blocks, chunk), flip, table, gu, quant_codes, quant_exps, down_rows
            )
            hqs.append(hq)
        outs[chunks[0]] = last_project(grid[2], mm, down_rows)
        kept = {chunk: outs[chunk][0] for chunk in chunks}
        sent = {chunk: outs[chunk][1] for chunk in chunks}
        own = reduce_to_owner(grid, group, kept, sent)
        turned = turn(hqs)
        projected, _ = gather(grid, own)
        return gram(turned, sum((chunk_blocks(projected, chunk) for chunk in chunks), []))

    placed = (
        P(("dom", "tok"), None),
        P(),
        P("dom", None, "tok"),
        P("dom", None, "tok"),
        P("dom", None, "tok"),
        P(("dom", "tok"), None),
    )
    return jax.shard_map(
        per_device, mesh=mesh, in_specs=placed, out_specs=P(("dom", "tok"), None), check_vma=False
    )
```
